256 devices in a mesh: row: 32 (over y, z), col: 8 (over x, core).
Axes of the slice: x: 4, y: 4, z: 8, core: 2. Of those that a mesh axis runs over, the one named last changes fastest.
Arguments:
- panel: float32 [8, 32, 256, 256], P(None, 'row', None, 'col'), may hold values from -0.1875 to 0.1875
- slab: bfloat16 [8, 32, 256, 4, 8, 256], P(None, 'row', None, None, 'col'), may hold values from -6 to 6
- cotangent: bfloat16 [8, 32, 256, 4, 8, 256], P(None, 'row', None, None, 'col'), may hold values from -0.0625 to 0.0625
- inverse: float32 [256, 256], replicated, may hold values from -2 to 8, as said below
Outputs:
- updated: bfloat16 [8, 32, 256, 4, 8, 256], P(None, 'row', None, None, 'col')
- grad_panel: float32 [8, 32, 256, 256], P(None, 'row', None, 'col')
- grad_inverse: float32 [256, 256], P(None, 'col')
The draws below stay inside these ranges and needn't reach their ends.
Inputs may be any that keep to these rules, and one draw needn't show every extreme that they name: `inverse`: lower triangular; diagonal entries between 4 and 8.
All inputs are finite; a program needn't handle non-finite values.
Results may differ from the reference program's by a relative error of at most 0.015.
Values may be sent and summed in bfloat16 or wider, within the bound.
A program may use at most 128 MiB of HBM per device.

```python
import jax
import jax.numpy as jnp
from jax import lax

TILE = 256
TR_DEV = 8
TC_DEV = 4
N_ROW = 32
N_COL = 8


def draw_inverse(key, part):
    key_diag = jax.random.fold_in(key, 11)
    key_off = jax.random.fold_in(key, 12)
    diag_vals = jax.random.uniform(key_diag, (TILE,), jnp.float32, 4.0, 8.0)
    off_vals = jnp.clip(0.25 * jax.random.normal(key_off, (TILE, TILE), jnp.float32), -1.5, 1.5)
    lower = jnp.tril(off_vals, -1)
    return (lower + jnp.diag(diag_vals)).astype(jnp.float32)


def level_of(key, extent, shards, least, largest):
    factor_of, own = 1.0, jax.random.fold_in(key, 6)
    for position, parts in shards:
        steps = jnp.exp(jax.random.uniform(jax.random.fold_in(own, position), (parts,), jnp.float32, least / len(shards), largest / len(shards)))
        factor_of = factor_of * jnp.repeat(steps, extent[position] // parts).reshape([-1 if axis == position else 1 for axis in range(len(extent))])
    return factor_of


def noise(rng, extent, deviation, bound, cuts=(), kind=jnp.bfloat16):
    level = level_of(rng, extent, cuts, -0.22, 0.18) if cuts else 1.0
    result = jax.random.normal(rng, extent, jnp.float32) * deviation * level
    return jnp.minimum(jnp.maximum(result, -bound), bound).astype(kind)


def setup_inputs(seed: int = 0) -> dict:
    streams_of = jax.random.split(jax.random.key(seed), 5)
    panel = noise(streams_of[0], (TR_DEV, N_ROW, TILE, TILE), 0.03, 0.1875, ((1, 32), (3, 8)), jnp.float32)
    slab = noise(streams_of[1], (TR_DEV, N_ROW, TILE, TC_DEV, N_COL, TILE), 1.0, 6.0, ((1, 32), (4, 8)))
    cotangent = noise(streams_of[2], (TR_DEV, N_ROW, TILE, TC_DEV, N_COL, TILE), 0.01, 0.0625, ((1, 32), (4, 8)))
    inverse = draw_inverse(jax.random.fold_in(streams_of[4], 71), 0)
    return {"panel": panel, "slab": slab, "cotangent": cotangent, "inverse": inverse}


def reference(panel, slab, cotangent, inverse):
    row_count = TR_DEV * N_ROW * TILE
    slab_width = TC_DEV * N_COL * TILE
    highest = lax.Precision.HIGHEST
    panel_rows = panel.reshape(row_count, TILE)
    factor = jnp.dot(panel_rows, inverse.T, precision=highest, preferred_element_type=jnp.float32)
    rounded = factor.astype(jnp.bfloat16)
    top_rows = rounded[:slab_width]
    slab_rows = slab.reshape(row_count, slab_width)
    product = jnp.dot(rounded, top_rows.T, preferred_element_type=jnp.float32)
    updated = (slab_rows.astype(jnp.float32) - product).astype(jnp.bfloat16)
    cot_rows = cotangent.reshape(row_count, slab_width)
    factor_grad = -jnp.dot(cot_rows, top_rows, preferred_element_type=jnp.float32)
    slab_grad = -jnp.dot(cot_rows.T, rounded, preferred_element_type=jnp.float32)
    factor_grad = factor_grad.at[:slab_width].add(slab_grad)
    grad_panel = jnp.dot(factor_grad, inverse, precision=highest, preferred_element_type=jnp.float32)
    grad_inverse = jnp.dot(factor_grad.T, panel_rows, precision=highest, preferred_element_type=jnp.float32)
    return updated.reshape(slab.shape), grad_panel.reshape(panel.shape), grad_inverse
```

```python
import jax
import jax.numpy as jnp
from jax import lax
from jax.experimental import pallas as pl
from jax.experimental.pallas import tpu as pltpu
from jax.sharding import PartitionSpec as P

BF = jnp.bfloat16
F32 = jnp.float32
ANY = pl.ANY
MESH = pl.DeviceIdType.MESH


S_A1, S_A2, S_B1, S_B2, S_B3 = 0, 4, 8, 9, 17
S_E1, S_E2, S_E3 = 21, 25, 33
S_D1, S_D2, S_DG = 41, 44, 56
S_GY, S_GZ = 57, 61
N_SEM = 72


def nn(a, b):
    return jnp.dot(a, b, preferred_element_type=F32)


def nt(a, b):
    return lax.dot_general(a, b, (((1,), (1,)), ((), ())), preferred_element_type=F32)


def halves(value):
    high = value.astype(BF)
    return high, (value - high.astype(F32)).astype(BF)


def kernel(
    panel_ref, slab_ref, cot_ref, inv_ref, upd_ref, gp_ref, gi_ref,
    strip, inv, inv_hi, inv_lo, invt_hi, invt_lo, perm, permt,
    graw, gs, sraw, pt, ft, fn, bpt, topt,
    et_own, et_send, e1, e2s, e2r, piece, zpiece, e3, e3s, esum,
    fgt0, gi, mst, d1, cmb, d2, gpo, gd1, gc, gd2, gyr, gzr, gio,
    ssem, rsem, lsem,
):
    row = lax.axis_index("row")
    col = lax.axis_index("col")
    y, z = row // 8, row % 8
    x, core = col // 2, col % 2
    twin = x * 2 + (1 - core)
    is_root = z == col
    mirror = y * 8 + col

    def x_at(d):
        return (x + d) % 4

    def col_at(d):
        return x_at(d) * 2 + core

    def row_y(d):
        return ((y + d) % 4) * 8 + z

    def row_z(d):
        return y * 8 + (z + d) % 8

    def remote(src, dst, send, recv, to_row, to_col):
        return pltpu.make_async_remote_copy(
            src_ref=src, dst_ref=dst, send_sem=ssem.at[send], recv_sem=rsem.at[recv],
            device_id=(to_row, to_col), device_id_type=MESH,
        )

    in_panel = pltpu.make_async_copy(panel_ref, strip, lsem.at[0])
    in_inv = pltpu.make_async_copy(inv_ref, inv, lsem.at[1])
    in_cot = pltpu.make_async_copy(cot_ref, graw, lsem.at[2])
    in_slab = pltpu.make_async_copy(slab_ref, sraw, lsem.at[3])
    in_panel.start()
    in_inv.start()
    in_cot.start()
    in_slab.start()

    barrier = pltpu.get_barrier_semaphore()

    def hello(to_row, to_col):
        pl.semaphore_signal(barrier, inc=1, device_id=(to_row, to_col), device_id_type=MESH)

    hello(row, twin)
    for d in range(1, 4):
        hello(row, col_at(d))
        hello(row_y(d), col)
    for d in range(1, 8):
        hello(row_z(d), col)

    @pl.when(jnp.logical_not(is_root))
    def _():
        hello(mirror, z)

    in_panel.wait()
    for k in range(8):
        pt[k, col] = strip[k].astype(BF)

    pl.semaphore_wait(barrier, 15 - is_root.astype(jnp.int32))

    b1 = remote(pt.at[0, col], bpt.at[col], S_B1, S_B1, mirror, z)
    b1_in = remote(pt.at[0, col], bpt.at[z], S_B1, S_B1, mirror, z)

    @pl.when(jnp.logical_not(is_root))
    def _():
        b1.start()

    @pl.when(is_root)
    def _():
        bpt[z] = pt[0, col]

    a1 = [remote(pt.at[:, col], pt.at[:, col], S_A1 + d, S_A1 + d, row, col_at(d)) for d in range(1, 4)]
    a1.append(remote(pt.at[:, col], pt.at[:, col], S_A1, S_A1, row, twin))
    for copy in a1:
        copy.start()

    in_inv.wait()
    inv_hi[...], inv_lo[...] = halves(inv[...])
    invt_hi[...], invt_lo[...] = halves(inv[...].T)
    r = lax.broadcasted_iota(jnp.int32, (256, 256), 0)
    q = lax.broadcasted_iota(jnp.int32, (256, 256), 1)
    perm[...] = jnp.where(q == (r % 64) * 4 + r // 64, 1.0, 0.0).astype(BF)
    permt[...] = jnp.where(r == (q % 64) * 4 + q // 64, 1.0, 0.0).astype(BF)
    zpiece[...] = jnp.zeros_like(zpiece)
    gi[...] = jnp.zeros_like(gi)

    @pl.when(jnp.logical_not(is_root))
    def _():
        b1_in.wait_recv()

    b2 = [remote(bpt.at[z], bpt.at[z], S_B2 + d, S_B2 + d, row_z(d), col) for d in range(1, 8)]
    for copy in b2:
        copy.start()

    a2 = []
    for d in range(1, 4):
        origin = x_at(4 - d) * 2 + core
        remote(pt.at[:, origin], pt.at[:, origin], S_A1 + d, S_A1 + d, row, col_at(d)).wait_recv()
        copy = remote(pt.at[:, origin], pt.at[:, origin], S_A2 + d, S_A2 + d, row, twin)
        copy.start()
        a2.append(copy)

    in_cot.wait()

    def split_columns(t, carry):
        block = graw[pl.ds(t * 64, 64)].reshape(256, 256)
        moved = nn(perm[...], block).astype(BF)
        for j in range(4):
            gs[j, pl.ds(t * 64, 64), :] = moved[j * 64 : (j + 1) * 64]
        return carry

    lax.fori_loop(0, 16, split_columns, 0)

    for d in range(1, 8):
        origin = (z + 8 - d) % 8
        remote(bpt.at[origin], bpt.at[origin], S_B2 + d, S_B2 + d, row_z(d), col).wait_recv()
    own_top = bpt[...].reshape(256, 256)
    topt[y] = (nn(inv_hi[...], own_top) + nn(inv_lo[...], own_top)).astype(BF)
    b3 = [remote(topt.at[y], topt.at[y], S_B3 + d, S_B3 + d, row_y(d), col) for d in range(1, 4)]
    for copy in b3:
        copy.start()

    remote(pt.at[:, twin], pt.at[:, twin], S_A1, S_A1, row, twin).wait_recv()
    for d in range(1, 4):
        origin = x_at(4 - d) * 2 + (1 - core)
        remote(pt.at[:, origin], pt.at[:, origin], S_A2 + d, S_A2 + d, row, twin).wait_recv()

    def factor_tile(k, carry):
        tile = pt[k].reshape(256, 256)
        value = nn(inv_hi[...], tile) + nn(inv_lo[...], tile)
        ft[k] = value.astype(BF)
        fn[k] = value.T.astype(BF)
        return carry

    lax.fori_loop(0, 8, factor_tile, 0)
    lax.fori_loop(16, 32, split_columns, 0)

    def column_sum(j):
        total = nn(ft[0], gs[j, 0:256, :])
        for k in range(1, 8):
            total += nn(ft[k], gs[j, k * 256 : (k + 1) * 256, :])
        return total

    e1_out = []
    for d in range(1, 4):
        other = (y + d) % 4
        et_send[d] = column_sum(other).astype(BF)
        copy = remote(et_send.at[d], e1.at[d], S_E1 + d, S_E1 + d, row_y(d), col)
        copy.start()
        e1_out.append(copy)
    et_own[...] = column_sum(y)

    for d in range(1, 4):
        origin = (y + 4 - d) % 4
        remote(topt.at[origin], topt.at[origin], S_B3 + d, S_B3 + d, row_y(d), col).wait_recv()

    def gradient_tile(k):
        start = pl.multiple_of(k * 256, 256)
        total = nt(topt[0], gs[0, pl.ds(start, 256), :])
        for j in range(1, 4):
            total += nt(topt[j], gs[j, pl.ds(start, 256), :])
        return -total

    def inverse_term(tile, high, low):
        return (nt(tile, high) + nt(tile, low)).reshape(4, 2, 32, 256)

    def times_inverse(k, high, low):
        value = nn(invt_hi[...], high) + nn(invt_hi[...], low) + nn(invt_lo[...], high)
        mst[k] = value.reshape(4, 2, 32, 256).astype(BF)

    def gradient_step(k, carry):
        high, low = halves(gradient_tile(k))
        gi[...] += inverse_term(pt[k].reshape(256, 256), high, low)
        times_inverse(k, high, low)
        return carry

    lax.fori_loop(1, 8, gradient_step, 0)
    d1_out = [remote(mst.at[pl.ds(1, 7), :, 1 - core], d1.at[pl.ds(1, 7)], S_D1, S_D1, row, twin)]
    d1_out[0].start()
    first = gradient_tile(0)
    fgt0[...] = first
    first_hi, first_lo = halves(first)
    gi[...] += inverse_term(pt[0].reshape(256, 256), first_hi, first_lo)

    for d in range(1, 4):
        remote(et_send.at[d], e1.at[d], S_E1 + d, S_E1 + d, row_y(d), col).wait_recv()
    total = et_own[...]
    for d in range(1, 4):
        total += e1[d].astype(F32)
    et_own[...] = total
    e2s[...] = total.reshape(8, 32, 256).astype(BF)
    e2_out = [
        remote(e2s.at[(z + d) % 8], e2r.at[d], S_E2 + d, S_E2 + d, row_z(d), col) for d in range(1, 8)
    ]
    for copy in e2_out:
        copy.start()

    def update_tile(k):
        start = pl.multiple_of(k * 256, 256)
        products = [nn(fn[k], topt[j]) for j in range(4)]
        for t in range(4):
            rows = pl.ds(pl.multiple_of(start + t * 64, 64), 64)
            old = nn(perm[...], sraw[rows].reshape(256, 256))
            new = jnp.concatenate(
                [old[j * 64 : (j + 1) * 64] - products[j][t * 64 : (t + 1) * 64] for j in range(4)], axis=0
            ).astype(BF)
            sraw[rows] = nn(permt[...], new).astype(BF).reshape(64, 4, 256)
        pltpu.make_async_copy(sraw.at[pl.ds(start, 256)], upd_ref.at[pl.ds(start, 256)], lsem.at[4 + k]).start()

    in_slab.wait()
    for k in range(3):
        update_tile(k)

    for d in range(1, 8):
        remote(e2s.at[(z + d) % 8], e2r.at[d], S_E2 + d, S_E2 + d, row_z(d), col).wait_recv()
    mine = pl.ds(pl.multiple_of(z * 32, 32), 32)
    total = et_own[mine, :]
    for d in range(1, 8):
        total += e2r[d].astype(F32)
    total = -total
    e3s[...] = total.astype(BF)
    away = (col - z + 8) % 8
    e3_out = remote(e3s, e3.at[z], S_E3, S_E3 + away, y * 8 + col, col)

    @pl.when(jnp.logical_not(is_root))
    def _():
        e3_out.start()

    zpiece[mine, :] = total
    piece_hi, piece_lo = halves(zpiece[...])
    gi[...] += inverse_term(bpt[...].reshape(256, 256), piece_hi, piece_lo)
    dg_out = remote(gi.at[:, 1 - core], gd1, S_DG, S_DG, row, twin)
    dg_out.start()

    def join(lo_k, hi_k):
        for other in range(4):
            for k in range(lo_k, hi_k):
                cmb[other, k] = (mst[k, other, core].astype(F32) + d1[k, other].astype(F32)).astype(BF)

    remote(mst.at[pl.ds(1, 7), :, 1 - core], d1.at[pl.ds(1, 7)], S_D1, S_D1, row, twin).wait_recv()
    join(1, 8)
    d2_out = []
    for d in range(1, 4):
        copy = remote(
            cmb.at[x_at(d), pl.ds(1, 7)], d2.at[d, pl.ds(1, 7)], S_D2 + d, S_D2 + d, row, col_at(d)
        )
        copy.start()
        d2_out.append(copy)

    @pl.when(is_root)
    def _():
        esum[z] = e3s[...]
        for d in range(1, 8):
            origin = (z + 8 - d) % 8
            remote(e3s, e3.at[origin], S_E3, S_E3 + d, row_z(d), col).wait_recv()
            esum[origin] = e3[origin]
        fgt0[...] += esum[...].reshape(256, 256).astype(F32)

    first_hi, first_lo = halves(fgt0[...])
    times_inverse(0, first_hi, first_lo)
    d1_out.append(remote(mst.at[0, :, 1 - core], d1.at[0], S_D1 + 1, S_D1 + 1, row, twin))
    d1_out[1].start()

    dg_out.wait_recv()
    gc[...] = gi[:, core] + gd1[...]
    for d in range(1, 4):
        copy = remote(gc.at[x_at(d)], gd2.at[d], S_D2 + 8 + d, S_D2 + 8 + d, row, col_at(d))
        copy.start()
        d2_out.append(copy)

    update_tile(3)

    d1_out[1].wait_recv()
    join(0, 1)
    for d in range(1, 4):
        copy = remote(cmb.at[x_at(d), 0], d2.at[d, 0], S_D2 + 4 + d, S_D2 + 4 + d, row, col_at(d))
        copy.start()
        d2_out.append(copy)

    for d in range(1, 4):
        remote(gc.at[x_at(d)], gd2.at[d], S_D2 + 8 + d, S_D2 + 8 + d, row, col_at(d)).wait_recv()
    gyr[y] = gc[x] + gd2[1] + gd2[2] + gd2[3]
    gy_out = [remote(gyr.at[y], gyr.at[y], S_GY + d, S_GY + d, row_y(d), col) for d in range(1, 4)]
    for copy in gy_out:
        copy.start()

    update_tile(4)
    update_tile(5)

    for d in range(1, 4):
        origin = (y + 4 - d) % 4
        remote(gyr.at[origin], gyr.at[origin], S_GY + d, S_GY + d, row_y(d), col).wait_recv()
    gzr[z] = gyr[0] + gyr[1] + gyr[2] + gyr[3]
    gz_out = [remote(gzr.at[z], gzr.at[z], S_GZ + d, S_GZ + d, row_z(d), col) for d in range(1, 8)]
    for copy in gz_out:
        copy.start()

    update_tile(6)
    update_tile(7)

    def finish(k):
        value = mst[k, x, core].astype(F32) + d1[k, x].astype(F32)
        for d in range(1, 4):
            value += d2[d, k].astype(F32)
        gpo[k] = value

    for d in range(1, 4):
        remote(
            cmb.at[x_at(d), pl.ds(1, 7)], d2.at[d, pl.ds(1, 7)], S_D2 + d, S_D2 + d, row, col_at(d)
        ).wait_recv()
    for k in range(1, 8):
        finish(k)
    for d in range(1, 4):
        remote(cmb.at[x_at(d), 0], d2.at[d, 0], S_D2 + 4 + d, S_D2 + 4 + d, row, col_at(d)).wait_recv()
    finish(0)
    out_gp = pltpu.make_async_copy(gpo, gp_ref, lsem.at[12])
    out_gp.start()

    for d in range(1, 8):
        origin = (z + 8 - d) % 8
        remote(gzr.at[origin], gzr.at[origin], S_GZ + d, S_GZ + d, row_z(d), col).wait_recv()
    total = gzr[0]
    for k in range(1, 8):
        total += gzr[k]
    gio[...] = total
    out_gi = pltpu.make_async_copy(gio, gi_ref, lsem.at[13])
    out_gi.start()

    @pl.when(jnp.logical_not(is_root))
    def _():
        b1.wait_send()
        e3_out.wait_send()

    for copy in a1 + a2 + b2 + b3 + e1_out + e2_out + d1_out + [dg_out] + d2_out + gy_out + gz_out:
        copy.wait_send()
    for k in range(8):
        rows = pl.ds(k * 256, 256)
        pltpu.make_async_copy(sraw.at[rows], upd_ref.at[rows], lsem.at[4 + k]).wait()
    out_gp.wait()
    out_gi.wait()


def per_device(panel, slab, cotangent, inverse):
    strips = jnp.transpose(panel.reshape(8, 256, 32), (0, 2, 1))
    vmem = pltpu.VMEM
    updated, grad_panel, grad_inverse = pl.pallas_call(
        kernel,
        out_shape=(
            jax.ShapeDtypeStruct((2048, 4, 256), BF),
            jax.ShapeDtypeStruct((8, 32, 256), F32),
            jax.ShapeDtypeStruct((32, 256), F32),
        ),
        in_specs=[pl.BlockSpec(memory_space=ANY)] * 4,
        out_specs=[pl.BlockSpec(memory_space=ANY)] * 3,
        scratch_shapes=[
            vmem((8, 32, 256), F32), vmem((256, 256), F32),
            vmem((256, 256), BF), vmem((256, 256), BF), vmem((256, 256), BF), vmem((256, 256), BF),
            vmem((256, 256), BF), vmem((256, 256), BF),
            vmem((2048, 4, 256), BF), vmem((4, 2048, 256), BF), vmem((2048, 4, 256), BF),
            vmem((8, 8, 32, 256), BF), vmem((8, 256, 256), BF), vmem((8, 256, 256), BF),
            vmem((8, 32, 256), BF), vmem((4, 256, 256), BF),
            vmem((256, 256), F32), vmem((4, 256, 256), BF), vmem((4, 256, 256), BF),
            vmem((8, 32, 256), BF), vmem((8, 32, 256), BF),
            vmem((32, 256), F32), vmem((256, 256), F32),
            vmem((8, 32, 256), BF), vmem((32, 256), BF), vmem((8, 32, 256), BF),
            vmem((256, 256), F32), vmem((4, 2, 32, 256), F32),
            vmem((8, 4, 2, 32, 256), BF), vmem((8, 4, 32, 256), BF),
            vmem((4, 8, 32, 256), BF), vmem((4, 8, 32, 256), BF),
            vmem((8, 32, 256), F32),
            vmem((4, 32, 256), F32), vmem((4, 32, 256), F32), vmem((4, 32, 256), F32),
            vmem((4, 32, 256), F32), vmem((8, 32, 256), F32), vmem((32, 256), F32),
            pltpu.SemaphoreType.DMA((N_SEM,)), pltpu.SemaphoreType.DMA((N_SEM,)), pltpu.SemaphoreType.DMA((16,)),
        ],
        compiler_params=pltpu.CompilerParams(
            collective_id=0, has_side_effects=True, vmem_limit_bytes=48 << 20
        ),
    )(strips, slab.reshape(2048, 4, 256), cotangent.reshape(2048, 4, 256), inverse)
    return (
        updated.reshape(slab.shape),
        jnp.transpose(grad_panel, (0, 2, 1)).reshape(panel.shape),
        jnp.transpose(grad_inverse),
    )


def solution(mesh):
    in_specs = (
        P(None, "row", None, "col"),
        P(None, "row", None, None, "col", None),
        P(None, "row", None, None, "col", None),
        P(),
    )
    out_specs = (
        P(None, "row", None, None, "col", None),
        P(None, "row", None, "col"),
        P(None, "col"),
    )
    return jax.shard_map(
        per_device, mesh=mesh, in_specs=in_specs, out_specs=out_specs, check_vma=False
    )
```

```python
import jax
import jax.numpy as jnp
from jax import lax
from jax.experimental import pallas as pl
from jax.experimental.pallas import tpu as pltpu
from jax.sharding import PartitionSpec as P

BF = jnp.bfloat16
F32 = jnp.float32
MESH = pl.DeviceIdType.MESH


S_A1, S_A2, S_B1, S_B2, S_B3 = 0, 8, 16, 17, 25
S_E1, S_E2, S_E3 = 29, 37, 45
S_D1, S_D2, S_WC, S_WX, S_WY, S_WZ = 46, 48, 56, 57, 61, 65
N_SEM = 73


def nn(a, b):
    return jnp.dot(a, b, preferred_element_type=F32)


def nt(a, b):
    return lax.dot_general(a, b, (((1,), (1,)), ((), ())), preferred_element_type=F32)


def halves(value):
    high = value.astype(BF)
    return high, (value - high.astype(F32)).astype(BF)


def three(high, low, other_high, other_low, product):
    return product(high, other_high) + product(high, other_low) + product(low, other_high)


def kernel(
    panel_ref, slab_ref, cot_ref, inv_ref, upd_ref, gp_ref, gi_ref,
    strip, inv, inv_hi, inv_lo, k_hi, k_lo, perm, permt,
    graw, gs, sraw, pt, fn, tp, topt,
    q_sum, n_own, n_send, e1, e2s, e2r, e3s, e3,
    r_hi, r_lo, w, mst, d1, cmb, d2, wd, wc, wx, wy, wz,
    ssem, rsem, lsem,
):
    row = lax.axis_index("row")
    col = lax.axis_index("col")
    y, z = row // 8, row % 8
    x, core = col // 2, col % 2
    twin = x * 2 + (1 - core)
    is_root = z == col
    mirror = y * 8 + col

    def x_at(d):
        return (x + d) % 4

    def col_at(d):
        return x_at(d) * 2 + core

    def row_y(d):
        return ((y + d) % 4) * 8 + z

    def row_z(d):
        return y * 8 + (z + d) % 8

    def remote(src, dst, send, recv, to_row, to_col):
        return pltpu.make_async_remote_copy(
            src_ref=src, dst_ref=dst, send_sem=ssem.at[send], recv_sem=rsem.at[recv],
            device_id=(to_row, to_col), device_id_type=MESH,
        )

    sent = []

    def send(src, dst, sem, to_row, to_col):
        copy = remote(src, dst, sem, sem, to_row, to_col)
        copy.start()
        sent.append(copy)

    def arrived(dst, sem):
        remote(dst, dst, sem, sem, row, twin).wait_recv()

    in_panel = pltpu.make_async_copy(panel_ref, strip, lsem.at[0])
    in_inv = pltpu.make_async_copy(inv_ref, inv, lsem.at[1])
    in_cot = pltpu.make_async_copy(cot_ref, graw, lsem.at[2])
    in_slab = pltpu.make_async_copy(slab_ref, sraw, lsem.at[3])
    in_panel.start()
    in_inv.start()
    in_cot.start()

    barrier = pltpu.get_barrier_semaphore()

    def hello(to_row, to_col):
        pl.semaphore_signal(barrier, inc=1, device_id=(to_row, to_col), device_id_type=MESH)

    hello(row, twin)
    for d in range(1, 4):
        hello(row, col_at(d))
        hello(row_y(d), col)
    for d in range(1, 8):
        hello(row_z(d), col)

    @pl.when(jnp.logical_not(is_root))
    def _():
        hello(mirror, z)

    in_panel.wait()
    for k in range(8):
        pt[k, col] = strip[k].astype(BF)

    pl.semaphore_wait(barrier, 15 - is_root.astype(jnp.int32))

    b1 = remote(pt.at[0, col], tp.at[y, col], S_B1, S_B1, mirror, z)

    @pl.when(jnp.logical_not(is_root))
    def _():
        b1.start()

    @pl.when(is_root)
    def _():
        tp[y, z] = pt[0, col]

    def half(h, c):
        return pt.at[pl.ds(4 * h, 4), c]

    for h in range(2):
        for d in (1, 3, 2):
            send(half(h, col), half(h, col), S_A1 + 4 * h + d, row, col_at(d))
        send(half(h, col), half(h, col), S_A1 + 4 * h, row, twin)
    in_slab.start()

    def pass_on(h, d):
        origin = x_at(4 - d) * 2 + core
        arrived(half(h, origin), S_A1 + 4 * h + d)
        send(half(h, origin), half(h, origin), S_A2 + 4 * h + d, row, twin)

    def to_other_y(piece):
        for d in range(1, 4):
            remote(tp.at[y, piece], tp.at[y, piece], S_B3 + d, S_B3 + d, row_y(d), col).start()

    def piece_from(d):
        origin = (z + 8 - d) % 8
        arrived(tp.at[y, origin], S_B2 + d)
        to_other_y(origin)

    r = lax.broadcasted_iota(jnp.int32, (256, 256), 0)
    q = lax.broadcasted_iota(jnp.int32, (256, 256), 1)
    perm[...] = jnp.where(q == (r % 64) * 4 + r // 64, 1.0, 0.0).astype(BF)
    permt[...] = jnp.where(r == (q % 64) * 4 + q // 64, 1.0, 0.0).astype(BF)

    in_cot.wait()

    def split_columns(t, carry):
        block = graw[pl.ds(t * 64, 64)].reshape(256, 256)
        moved = nn(perm[...], block).astype(BF)
        for j in range(4):
            gs[j, pl.ds(t * 64, 64), :] = moved[j * 64 : (j + 1) * 64]
        return carry

    @pl.when(jnp.logical_not(is_root))
    def _():
        arrived(tp.at[y, z], S_B1)

    for d in (4, 3, 5, 2, 6, 1, 7):
        send(tp.at[y, z], tp.at[y, z], S_B2 + d, row_z(d), col)
    to_other_y(z)

    lax.fori_loop(0, 4, split_columns, 0)
    pass_on(0, 1)
    pass_on(0, 3)
    piece_from(1)
    piece_from(7)
    lax.fori_loop(4, 8, split_columns, 0)
    pass_on(0, 2)
    piece_from(2)
    piece_from(6)
    lax.fori_loop(8, 14, split_columns, 0)
    pass_on(1, 1)
    pass_on(1, 3)
    piece_from(3)
    piece_from(5)
    lax.fori_loop(14, 18, split_columns, 0)
    piece_from(4)
    pass_on(1, 2)
    lax.fori_loop(18, 32, split_columns, 0)

    in_inv.wait()
    high, low = halves(inv[...])
    inv_hi[...], inv_lo[...] = high, low
    t_high, t_low = halves(inv[...].T)
    k_hi[...], k_lo[...] = halves(three(t_high, t_low, high, low, nn))

    def panel_half(h):
        arrived(half(h, twin), S_A1 + 4 * h)
        for d in range(1, 4):
            origin = x_at(4 - d) * 2 + (1 - core)
            arrived(half(h, origin), S_A2 + 4 * h + d)

    def row_sum(j, h):
        total = nn(pt[4 * h].reshape(256, 256), gs[j, pl.ds(4 * h * 256, 256), :])
        for k in range(4 * h + 1, 4 * h + 4):
            total += nn(pt[k].reshape(256, 256), gs[j, pl.ds(k * 256, 256), :])
        return total

    def first_rows(j, carry):
        q_sum[j] = row_sum(j, 0)
        return carry

    panel_half(0)
    lax.fori_loop(0, 4, first_rows, 0)
    panel_half(1)

    def times_k(value):
        high, low = halves(value)
        return three(k_hi[...], k_lo[...], high, low, nn)

    for d in (2, 1, 3):
        other = (y + d) % 4
        total = q_sum[other] + row_sum(other, 1)
        q_sum[other] = total
        n_send[d] = times_k(total).astype(BF)
        for h in range(2):
            rows = pl.ds(128 * h, 128)
            send(n_send.at[d, rows], e1.at[d, rows], S_E1 + 4 * h + d, row_y(d), col)
    total = q_sum[y] + row_sum(y, 1)
    q_sum[y] = total
    n_own[...] = times_k(total)

    for d in range(1, 4):
        arrived(tp.at[(y + 4 - d) % 4], S_B3 + d)

    def column_sum(t, carry):
        rows = pl.ds(pl.multiple_of(t * 256, 256), 256)
        total = nt(gs[0, rows, :], tp[0].reshape(256, 256))
        for j in range(1, 4):
            total += nt(gs[j, rows, :], tp[j].reshape(256, 256))
        high, low = halves(total)
        r_hi[rows, :] = high
        r_lo[rows, :] = low
        tile = pt[t].reshape(256, 256)
        w[...] += (nn(tile, high) + nn(tile, low)).reshape(4, 2, 32, 256)
        return carry

    total = jnp.zeros((256, 256), F32)
    for j in range(4):
        high, low = halves(q_sum[j])
        tile = tp[j].reshape(256, 256)
        total += nt(tile, high) + nt(tile, low)
    w[...] = total.reshape(4, 2, 32, 256)
    lax.fori_loop(0, 8, column_sum, 0)
    send(w.at[:, 1 - core], wd, S_WC, row, twin)

    def k_tile(k, carry):
        rows = pl.ds(pl.multiple_of(k * 256, 256), 256)
        value = three(k_hi[...], k_lo[...], r_hi[rows, :], r_lo[rows, :], nt)
        mst[k] = value.reshape(4, 2, 32, 256).astype(BF)
        return carry

    def core_half(h):
        send(mst.at[pl.ds(4 * h, 4), :, 1 - core], d1.at[pl.ds(4 * h, 4)], S_D1 + h, row, twin)

    def join(h):
        arrived(d1.at[pl.ds(4 * h, 4)], S_D1 + h)
        for other in range(4):
            for k in range(4 * h, 4 * h + 4):
                cmb[other, k] = (mst[k, other, core].astype(F32) + d1[k, other].astype(F32)).astype(BF)
        for d in (1, 3, 2):
            part = pl.ds(4 * h, 4)
            send(cmb.at[x_at(d), part], d2.at[d, part], S_D2 + 4 * h + d, row, col_at(d))

    def strips_out(h):
        rows = pl.ds(128 * h, 128)
        total = n_own[rows, :]
        for d in range(1, 4):
            arrived(e1.at[d, rows], S_E1 + 4 * h + d)
            total += e1[d, rows, :].astype(F32)
        n_own[rows, :] = total
        e2s[pl.ds(4 * h, 4)] = total.reshape(4, 32, 256).astype(BF)
        for other in range(4 * h, 4 * h + 4):

            @pl.when(z != other)
            def _():
                remote(e2s.at[other], e2r.at[z], S_E2 + other, S_E2 + z, y * 8 + other, col).start()

    lax.fori_loop(0, 4, k_tile, 0)
    core_half(0)

    arrived(wd, S_WC)
    wc[...] = w[:, core] + wd[...]
    for d in (2, 1, 3):
        send(wc.at[x_at(d)], wx.at[d], S_WX + d, row, col_at(d))

    lax.fori_loop(4, 8, k_tile, 0)
    core_half(1)
    join(0)
    strips_out(0)
    join(1)
    strips_out(1)

    for d in range(1, 4):
        arrived(wx.at[d], S_WX + d)
    total = (wc[x] + wx[1] + wx[2] + wx[3]).astype(BF)
    wy[y] = total
    for d in (2, 1, 3):
        send(wy.at[y], wy.at[y], S_WY + d, row_y(d), col)

    def top_tile(j, carry):
        tile = tp[j].reshape(256, 256)
        topt[j] = (nn(inv_hi[...], tile) + nn(inv_lo[...], tile)).astype(BF)
        return carry

    def factor_tile(k, carry):
        tile = pt[k].reshape(256, 256)
        fn[k] = (nn(inv_hi[...], tile) + nn(inv_lo[...], tile)).T.astype(BF)
        return carry

    lax.fori_loop(0, 4, top_tile, 0)
    lax.fori_loop(0, 4, factor_tile, 0)

    for d in range(1, 4):
        arrived(wy.at[(y + 4 - d) % 4], S_WY + d)
    total = wy[0].astype(F32)
    for k in range(1, 4):
        total += wy[k].astype(F32)
    wz[z] = total.astype(BF)
    for d in (4, 3, 5, 2, 6, 1, 7):
        send(wz.at[z], wz.at[z], S_WZ + d, row_z(d), col)

    for d in range(1, 8):
        origin = (z + 8 - d) % 8
        arrived(e2r.at[origin], S_E2 + origin)
    e2r[z] = jnp.zeros((32, 256), BF)
    total = n_own[pl.ds(pl.multiple_of(z * 32, 32), 32), :]
    for k in range(8):
        total += e2r[k].astype(F32)
    e3s[...] = total.astype(BF)
    e3_out = remote(e3s, e3, S_E3, S_E3, mirror, z)

    @pl.when(jnp.logical_not(is_root))
    def _():
        e3_out.start()

    lax.fori_loop(4, 8, factor_tile, 0)
    in_slab.wait()

    def update_tile(k, carry):
        start = pl.multiple_of(k * 256, 256)
        products = [nn(fn[k], topt[j]) for j in range(4)]
        for t in range(4):
            rows = pl.ds(pl.multiple_of(start + t * 64, 64), 64)
            old = nn(perm[...], sraw[rows].reshape(256, 256))
            new = jnp.concatenate(
                [old[j * 64 : (j + 1) * 64] - products[j][t * 64 : (t + 1) * 64] for j in range(4)], axis=0
            ).astype(BF)
            upd_ref[rows] = nn(permt[...], new).astype(BF).reshape(64, 4, 256)
        return carry

    lax.fori_loop(0, 8, update_tile, 0)

    for h in range(2):
        for d in range(1, 4):
            arrived(d2.at[d, pl.ds(4 * h, 4)], S_D2 + 4 * h + d)
    for k in range(1, 8):
        value = mst[k, x, core].astype(F32) + d1[k, x].astype(F32)
        for d in range(1, 4):
            value += d2[d, k].astype(F32)
        gp_ref[k] = -value

    @pl.when(is_root)
    def _():
        e3[...] = e3s[...]

    @pl.when(jnp.logical_not(is_root))
    def _():
        arrived(e3, S_E3)

    value = mst[0, x, core].astype(F32) + d1[0, x].astype(F32) + e3[...].astype(F32)
    for d in range(1, 4):
        value += d2[d, 0].astype(F32)
    gp_ref[0] = -value

    for d in range(1, 8):
        arrived(wz.at[(z + 8 - d) % 8], S_WZ + d)
    total = wz[0].astype(F32)
    for k in range(1, 8):
        total += wz[k].astype(F32)
    high, low = halves(total)
    gi_ref[...] = -three(high, low, inv_hi[...], inv_lo[...], nt)

    @pl.when(jnp.logical_not(is_root))
    def _():
        b1.wait_send()
        e3_out.wait_send()

    for d in range(1, 4):
        remote(tp.at[y], tp.at[y], S_B3 + d, S_B3 + d, row_y(d), col).wait_send()
    for other in range(8):

        @pl.when(z != other)
        def _():
            remote(e2s.at[other], e2r.at[z], S_E2 + other, S_E2 + z, y * 8 + other, col).wait_send()

    for copy in sent:
        copy.wait_send()


def per_device(panel, slab, cotangent, inverse):
    strips = jnp.transpose(panel.reshape(8, 256, 32), (0, 2, 1))
    vmem = pltpu.VMEM
    updated, grad_panel, grad_inverse = pl.pallas_call(
        kernel,
        out_shape=(
            jax.ShapeDtypeStruct((2048, 4, 256), BF),
            jax.ShapeDtypeStruct((8, 32, 256), F32),
            jax.ShapeDtypeStruct((32, 256), F32),
        ),
        in_specs=[pl.BlockSpec(memory_space=pltpu.HBM)] * 4,
        out_specs=[pl.BlockSpec(memory_space=vmem)] * 3,
        scratch_shapes=[
            vmem((8, 32, 256), F32), vmem((256, 256), F32),
            vmem((256, 256), BF), vmem((256, 256), BF), vmem((256, 256), BF), vmem((256, 256), BF),
            vmem((256, 256), BF), vmem((256, 256), BF),
            vmem((2048, 4, 256), BF), vmem((4, 2048, 256), BF), vmem((2048, 4, 256), BF),
            vmem((8, 8, 32, 256), BF), vmem((8, 256, 256), BF),
            vmem((4, 8, 32, 256), BF), vmem((4, 256, 256), BF),
            vmem((4, 256, 256), F32), vmem((256, 256), F32),
            vmem((4, 256, 256), BF), vmem((4, 256, 256), BF),
            vmem((8, 32, 256), BF), vmem((8, 32, 256), BF),
            vmem((32, 256), BF), vmem((32, 256), BF),
            vmem((2048, 256), BF), vmem((2048, 256), BF), vmem((4, 2, 32, 256), F32),
            vmem((8, 4, 2, 32, 256), BF), vmem((8, 4, 32, 256), BF),
            vmem((4, 8, 32, 256), BF), vmem((4, 8, 32, 256), BF),
            vmem((4, 32, 256), F32), vmem((4, 32, 256), F32), vmem((4, 32, 256), F32),
            vmem((4, 32, 256), BF), vmem((8, 32, 256), BF),
            pltpu.SemaphoreType.DMA((N_SEM,)), pltpu.SemaphoreType.DMA((N_SEM,)), pltpu.SemaphoreType.DMA((4,)),
        ],
        compiler_params=pltpu.CompilerParams(
            collective_id=0, has_side_effects=True, vmem_limit_bytes=48 << 20
        ),
    )(strips, slab.reshape(2048, 4, 256), cotangent.reshape(2048, 4, 256), inverse)
    return (
        updated.reshape(slab.shape),
        jnp.transpose(grad_panel, (0, 2, 1)).reshape(panel.shape),
        jnp.transpose(grad_inverse),
    )


def solution(mesh):
    in_specs = (
        P(None, "row", None, "col"),
        P(None, "row", None, None, "col", None),
        P(None, "row", None, None, "col", None),
        P(),
    )
    out_specs = (
        P(None, "row", None, None, "col", None),
        P(None, "row", None, "col"),
        P(None, "col"),
    )
    return jax.shard_map(
        per_device, mesh=mesh, in_specs=in_specs, out_specs=out_specs, check_vma=False
    )
```

```python
import jax
import jax.numpy as jnp
from jax import lax
from jax.experimental import pallas as pl
from jax.experimental.pallas import tpu as pltpu
from jax.sharding import PartitionSpec as P

BF = jnp.bfloat16
F32 = jnp.float32
MESH = pl.DeviceIdType.MESH


S_A1, S_A2, S_B1, S_B2, S_B3 = 0, 8, 16, 17, 25
S_E1, S_E2, S_E3 = 29, 37, 45
S_D1, S_D2, S_WC, S_WX, S_WY, S_WZ = 46, 48, 56, 57, 61, 65
N_SEM = 73


def nn(a, b):
    return jnp.dot(a, b, preferred_element_type=F32)


def nt(a, b):
    return lax.dot_general(a, b, (((1,), (1,)), ((), ())), preferred_element_type=F32)


def halves(value):
    high = value.astype(BF)
    return high, (value - high.astype(F32)).astype(BF)


def three(high, low, other_high, other_low, product):
    return product(high, other_high) + product(high, other_low) + product(low, other_high)


def kernel(
    panel_ref, slab_ref, cot_ref, inv_ref, upd_ref, gp_ref, gi_ref,
    strip, inv, inv_hi, inv_lo, k_hi, k_lo, perm, permt,
    graw, gs, sraw, pt, fn, tp, topt,
    q_sum, q_bf, n_own, n_send, e1, e2s, e2r, e3s, e3,
    r_bf, w, mst, d1, cmb, d2, wd, wc, wx, wy, wz, gpo, gio,
    ssem, rsem, lsem,
):
    row = lax.axis_index("row")
    col = lax.axis_index("col")
    y, z = row // 8, row % 8
    x, core = col // 2, col % 2
    twin = x * 2 + (1 - core)
    is_root = z == col
    mirror = y * 8 + col

    def x_at(d):
        return (x + d) % 4

    def col_at(d):
        return x_at(d) * 2 + core

    def row_y(d):
        return ((y + d) % 4) * 8 + z

    def row_z(d):
        return y * 8 + (z + d) % 8

    def remote(src, dst, send, recv, to_row, to_col):
        return pltpu.make_async_remote_copy(
            src_ref=src, dst_ref=dst, send_sem=ssem.at[send], recv_sem=rsem.at[recv],
            device_id=(to_row, to_col), device_id_type=MESH,
        )

    sent = []

    def send(src, dst, sem, to_row, to_col):
        copy = remote(src, dst, sem, sem, to_row, to_col)
        copy.start()
        sent.append(copy)

    def arrived(dst, sem):
        remote(dst, dst, sem, sem, row, twin).wait_recv()

    in_panel = pltpu.make_async_copy(panel_ref, strip, lsem.at[0])
    in_inv = pltpu.make_async_copy(inv_ref, inv, lsem.at[1])
    in_cot = pltpu.make_async_copy(cot_ref, graw, lsem.at[2])
    in_slab = pltpu.make_async_copy(slab_ref, sraw, lsem.at[3])
    in_panel.start()
    in_inv.start()
    in_cot.start()

    barrier = pltpu.get_barrier_semaphore()

    def hello(to_row, to_col):
        pl.semaphore_signal(barrier, inc=1, device_id=(to_row, to_col), device_id_type=MESH)

    hello(row, twin)
    for d in range(1, 4):
        hello(row, col_at(d))
        hello(row_y(d), col)
    for d in range(1, 8):
        hello(row_z(d), col)

    @pl.when(jnp.logical_not(is_root))
    def _():
        hello(mirror, z)

    in_panel.wait()
    for k in range(8):
        pt[k, col] = strip[k].astype(BF)

    r = lax.broadcasted_iota(jnp.int32, (256, 256), 0)
    q = lax.broadcasted_iota(jnp.int32, (256, 256), 1)
    perm[...] = jnp.where(q == (r % 64) * 4 + r // 64, 1.0, 0.0).astype(BF)
    permt[...] = jnp.where(r == (q % 64) * 4 + q // 64, 1.0, 0.0).astype(BF)
    in_inv.wait()
    high, low = halves(inv[...])
    inv_hi[...], inv_lo[...] = high, low
    t_high, t_low = halves(inv[...].T)
    k_hi[...], k_lo[...] = halves(three(t_high, t_low, high, low, nn))

    pl.semaphore_wait(barrier, 15 - is_root.astype(jnp.int32))

    b1 = remote(pt.at[0, col], tp.at[y, col], S_B1, S_B1, mirror, z)

    @pl.when(jnp.logical_not(is_root))
    def _():
        b1.start()

    @pl.when(is_root)
    def _():
        tp[y, z] = pt[0, col]

    def half(h, c):
        return pt.at[pl.ds(4 * h, 4), c]

    for h in range(2):
        for d in (1, 3, 2):
            send(half(h, col), half(h, col), S_A1 + 4 * h + d, row, col_at(d))
        send(half(h, col), half(h, col), S_A1 + 4 * h, row, twin)
    in_slab.start()

    def pass_on(h, d):
        origin = x_at(4 - d) * 2 + core
        arrived(half(h, origin), S_A1 + 4 * h + d)
        send(half(h, origin), half(h, origin), S_A2 + 4 * h + d, row, twin)

    def to_other_y(piece):
        for d in range(1, 4):
            remote(tp.at[y, piece], tp.at[y, piece], S_B3 + d, S_B3 + d, row_y(d), col).start()

    def piece_from(d):
        origin = (z + 8 - d) % 8
        arrived(tp.at[y, origin], S_B2 + d)
        to_other_y(origin)

    in_cot.wait()

    def split_columns(t, carry):
        block = graw[pl.ds(t * 64, 64)].reshape(256, 256)
        moved = nn(perm[...], block).astype(BF)
        for j in range(4):
            gs[pl.ds(t * 64, 64), j * 256 : (j + 1) * 256] = moved[j * 64 : (j + 1) * 64]
        return carry

    @pl.when(jnp.logical_not(is_root))
    def _():
        arrived(tp.at[y, z], S_B1)

    for d in (4, 3, 5, 2, 6, 1, 7):
        send(tp.at[y, z], tp.at[y, z], S_B2 + d, row_z(d), col)
    to_other_y(z)

    lax.fori_loop(0, 4, split_columns, 0, unroll=2)
    pass_on(0, 1)
    pass_on(0, 3)
    piece_from(1)
    piece_from(7)
    lax.fori_loop(4, 8, split_columns, 0, unroll=2)
    pass_on(0, 2)
    piece_from(2)
    piece_from(6)
    lax.fori_loop(8, 14, split_columns, 0, unroll=2)
    pass_on(1, 1)
    pass_on(1, 3)
    piece_from(3)
    piece_from(5)
    lax.fori_loop(14, 18, split_columns, 0, unroll=2)
    piece_from(4)
    pass_on(1, 2)
    lax.fori_loop(18, 32, split_columns, 0, unroll=2)

    def panel_half(h):
        arrived(half(h, twin), S_A1 + 4 * h)
        for d in range(1, 4):
            origin = x_at(4 - d) * 2 + (1 - core)
            arrived(half(h, origin), S_A2 + 4 * h + d)

    def panel_rows(k0, k1):
        return jnp.concatenate([pt[k].reshape(256, 256) for k in range(k0, k1)], axis=1)

    panel_half(0)
    q_sum[...] = nn(panel_rows(0, 4), gs[0:1024, :])
    panel_half(1)

    def column_tile(j):
        columns = pl.ds(pl.multiple_of(j * 256, 256), 256)
        total = (q_sum[:, columns] + nn(panel_rows(4, 8), gs[1024:2048, columns])).astype(BF)
        q_bf[j] = total
        return nn(k_hi[...], total) + nn(k_lo[...], total)

    for d in (2, 1, 3):
        n_send[d] = column_tile((y + d) % 4).astype(BF)
        for h in range(2):
            rows = pl.ds(128 * h, 128)
            send(n_send.at[d, rows], e1.at[d, rows], S_E1 + 4 * h + d, row_y(d), col)
    n_own[...] = column_tile(y)

    for d in range(1, 4):
        arrived(tp.at[(y + 4 - d) % 4], S_B3 + d)

    def top_columns():
        return jnp.concatenate([tp[j].reshape(256, 256) for j in range(4)], axis=1)

    def column_sum(t, carry):
        rows = pl.ds(pl.multiple_of(t * 512, 512), 512)
        r_bf[rows, :] = nt(gs[rows, :], top_columns()).astype(BF)
        return carry

    lax.fori_loop(0, 4, column_sum, 0)
    q_all = jnp.concatenate([q_bf[j] for j in range(4)], axis=1)
    w[...] = (nn(panel_rows(0, 8), r_bf[...]) + nt(top_columns(), q_all)).reshape(4, 2, 32, 256)
    send(w.at[:, 1 - core], wd, S_WC, row, twin)

    def k_tile(k, carry):
        rows = pl.ds(pl.multiple_of(k * 256, 256), 256)
        value = nt(k_hi[...], r_bf[rows, :]) + nt(k_lo[...], r_bf[rows, :])
        mst[k] = value.reshape(4, 2, 32, 256).astype(BF)
        return carry

    def core_half(h):
        send(mst.at[pl.ds(4 * h, 4), :, 1 - core], d1.at[pl.ds(4 * h, 4)], S_D1 + h, row, twin)

    def join(h):
        arrived(d1.at[pl.ds(4 * h, 4)], S_D1 + h)
        for other in range(4):
            for k in range(4 * h, 4 * h + 4):
                cmb[other, k] = (mst[k, other, core].astype(F32) + d1[k, other].astype(F32)).astype(BF)
        for d in (1, 3, 2):
            part = pl.ds(4 * h, 4)
            send(cmb.at[x_at(d), part], d2.at[d, part], S_D2 + 4 * h + d, row, col_at(d))

    def strips_out(h):
        rows = pl.ds(128 * h, 128)
        total = n_own[rows, :]
        for d in range(1, 4):
            arrived(e1.at[d, rows], S_E1 + 4 * h + d)
            total += e1[d, rows, :].astype(F32)
        n_own[rows, :] = total
        e2s[pl.ds(4 * h, 4)] = total.reshape(4, 32, 256).astype(BF)
        for other in range(4 * h, 4 * h + 4):

            @pl.when(z != other)
            def _():
                remote(e2s.at[other], e2r.at[z], S_E2 + other, S_E2 + z, y * 8 + other, col).start()

    lax.fori_loop(0, 4, k_tile, 0)
    core_half(0)

    arrived(wd, S_WC)
    wc[...] = w[:, core] + wd[...]
    for d in (2, 1, 3):
        send(wc.at[x_at(d)], wx.at[d], S_WX + d, row, col_at(d))

    lax.fori_loop(4, 8, k_tile, 0)
    core_half(1)
    join(0)
    strips_out(0)
    join(1)
    strips_out(1)

    for d in range(1, 4):
        arrived(wx.at[d], S_WX + d)
    total = (wc[x] + wx[1] + wx[2] + wx[3]).astype(BF)
    wy[y] = total
    for d in (2, 1, 3):
        send(wy.at[y], wy.at[y], S_WY + d, row_y(d), col)

    def top_tile(j, carry):
        tile = tp[j].reshape(256, 256)
        topt[j] = (nn(inv_hi[...], tile) + nn(inv_lo[...], tile)).astype(BF)
        return carry

    def factor_tile(k, carry):
        tile = pt[k].reshape(256, 256)
        fn[k] = (nn(inv_hi[...], tile) + nn(inv_lo[...], tile)).T.astype(BF)
        return carry

    lax.fori_loop(0, 4, top_tile, 0)
    lax.fori_loop(0, 4, factor_tile, 0)

    for d in range(1, 4):
        arrived(wy.at[(y + 4 - d) % 4], S_WY + d)
    total = wy[0].astype(F32)
    for k in range(1, 4):
        total += wy[k].astype(F32)
    wz[z] = total.astype(BF)
    for d in (4, 3, 5, 2, 6, 1, 7):
        send(wz.at[z], wz.at[z], S_WZ + d, row_z(d), col)

    for d in range(1, 8):
        origin = (z + 8 - d) % 8
        arrived(e2r.at[origin], S_E2 + origin)
    e2r[z] = jnp.zeros((32, 256), BF)
    total = n_own[pl.ds(pl.multiple_of(z * 32, 32), 32), :]
    for k in range(8):
        total += e2r[k].astype(F32)
    e3s[...] = total.astype(BF)
    e3_out = remote(e3s, e3, S_E3, S_E3, mirror, z)

    @pl.when(jnp.logical_not(is_root))
    def _():
        e3_out.start()

    lax.fori_loop(4, 8, factor_tile, 0)
    in_slab.wait()

    def out_rows(k):
        rows = pl.ds(pl.multiple_of(k * 256, 256), 256)
        return pltpu.make_async_copy(sraw.at[rows], upd_ref.at[rows], lsem.at[4 + k])

    def update_tile(k, carry):
        start = pl.multiple_of(k * 256, 256)
        products = [nn(fn[k], topt[j]).astype(BF) for j in range(4)]
        for t in range(4):
            rows = pl.ds(pl.multiple_of(start + t * 64, 64), 64)
            product = jnp.concatenate([products[j][t * 64 : (t + 1) * 64] for j in range(4)], axis=0)
            old = sraw[rows].reshape(256, 256).astype(F32)
            sraw[rows] = (old - nn(permt[...], product)).astype(BF).reshape(64, 4, 256)
        out_rows(k).start()
        return carry

    lax.fori_loop(0, 8, update_tile, 0)

    for h in range(2):
        for d in range(1, 4):
            arrived(d2.at[d, pl.ds(4 * h, 4)], S_D2 + 4 * h + d)
    for k in range(1, 8):
        value = mst[k, x, core].astype(F32) + d1[k, x].astype(F32)
        for d in range(1, 4):
            value += d2[d, k].astype(F32)
        gpo[k] = -value

    @pl.when(is_root)
    def _():
        e3[...] = e3s[...]

    @pl.when(jnp.logical_not(is_root))
    def _():
        arrived(e3, S_E3)

    value = mst[0, x, core].astype(F32) + d1[0, x].astype(F32) + e3[...].astype(F32)
    for d in range(1, 4):
        value += d2[d, 0].astype(F32)
    gpo[0] = -value
    out_gp = pltpu.make_async_copy(gpo, gp_ref, lsem.at[12])
    out_gp.start()

    for d in range(1, 8):
        arrived(wz.at[(z + 8 - d) % 8], S_WZ + d)
    total = wz[0].astype(F32)
    for k in range(1, 8):
        total += wz[k].astype(F32)
    high, low = halves(total)
    gio[...] = -three(high, low, inv_hi[...], inv_lo[...], nt)
    out_gi = pltpu.make_async_copy(gio, gi_ref, lsem.at[13])
    out_gi.start()

    @pl.when(jnp.logical_not(is_root))
    def _():
        b1.wait_send()
        e3_out.wait_send()

    for d in range(1, 4):
        remote(tp.at[y], tp.at[y], S_B3 + d, S_B3 + d, row_y(d), col).wait_send()
    for other in range(8):

        @pl.when(z != other)
        def _():
            remote(e2s.at[other], e2r.at[z], S_E2 + other, S_E2 + z, y * 8 + other, col).wait_send()

    for copy in sent:
        copy.wait_send()
    for k in range(8):
        out_rows(k).wait()
    out_gp.wait()
    out_gi.wait()


def per_device(panel, slab, cotangent, inverse):
    strips = jnp.transpose(panel.reshape(8, 256, 32), (0, 2, 1))
    vmem = pltpu.VMEM
    updated, grad_panel, grad_inverse = pl.pallas_call(
        kernel,
        out_shape=(
            jax.ShapeDtypeStruct((2048, 4, 256), BF),
            jax.ShapeDtypeStruct((8, 32, 256), F32),
            jax.ShapeDtypeStruct((32, 256), F32),
        ),
        in_specs=[pl.BlockSpec(memory_space=pltpu.HBM)] * 4,
        out_specs=[pl.BlockSpec(memory_space=pl.ANY)] * 3,
        scratch_shapes=[
            vmem((8, 32, 256), F32), vmem((256, 256), F32),
            vmem((256, 256), BF), vmem((256, 256), BF), vmem((256, 256), BF), vmem((256, 256), BF),
            vmem((256, 256), BF), vmem((256, 256), BF),
            vmem((2048, 4, 256), BF), vmem((2048, 1024), BF), vmem((2048, 4, 256), BF),
            vmem((8, 8, 32, 256), BF), vmem((8, 256, 256), BF),
            vmem((4, 8, 32, 256), BF), vmem((4, 256, 256), BF),
            vmem((256, 1024), F32), vmem((4, 256, 256), BF), vmem((256, 256), F32),
            vmem((4, 256, 256), BF), vmem((4, 256, 256), BF),
            vmem((8, 32, 256), BF), vmem((8, 32, 256), BF),
            vmem((32, 256), BF), vmem((32, 256), BF),
            vmem((2048, 256), BF), vmem((4, 2, 32, 256), F32),
            vmem((8, 4, 2, 32, 256), BF), vmem((8, 4, 32, 256), BF),
            vmem((4, 8, 32, 256), BF), vmem((4, 8, 32, 256), BF),
            vmem((4, 32, 256), F32), vmem((4, 32, 256), F32), vmem((4, 32, 256), F32),
            vmem((4, 32, 256), BF), vmem((8, 32, 256), BF),
            vmem((8, 32, 256), F32), vmem((32, 256), F32),
            pltpu.SemaphoreType.DMA((N_SEM,)), pltpu.SemaphoreType.DMA((N_SEM,)), pltpu.SemaphoreType.DMA((14,)),
        ],
        compiler_params=pltpu.CompilerParams(
            collective_id=0, has_side_effects=True, vmem_limit_bytes=56 << 20
        ),
    )(strips, slab.reshape(2048, 4, 256), cotangent.reshape(2048, 4, 256), inverse)
    return (
        updated.reshape(slab.shape),
        jnp.transpose(grad_panel, (0, 2, 1)).reshape(panel.shape),
        jnp.transpose(grad_inverse),
    )


def solution(mesh):
    in_specs = (
        P(None, "row", None, "col"),
        P(None, "row", None, None, "col", None),
        P(None, "row", None, None, "col", None),
        P(),
    )
    out_specs = (
        P(None, "row", None, None, "col", None),
        P(None, "row", None, "col"),
        P(None, "col"),
    )
    return jax.shard_map(
        per_device, mesh=mesh, in_specs=in_specs, out_specs=out_specs, check_vma=False
    )
```

```python
import jax
import jax.numpy as jnp
from jax import lax
from jax.experimental import pallas as pl
from jax.experimental.pallas import tpu as pltpu
from jax.sharding import PartitionSpec as P

BF = jnp.bfloat16
F32 = jnp.float32
MESH = pl.DeviceIdType.MESH


S_A1, S_A2, S_B2, S_B3 = 0, 8, 17, 25
S_E1, S_E2, S_E3 = 29, 37, 45
S_D1, S_D2, S_WC, S_WX, S_WY, S_WZ = 46, 48, 56, 57, 61, 65
N_SEM = 73


def nn(a, b):
    return jnp.dot(a, b, preferred_element_type=F32)


def nt(a, b):
    return lax.dot_general(a, b, (((1,), (1,)), ((), ())), preferred_element_type=F32)


def halves(value):
    high = value.astype(BF)
    return high, (value - high.astype(F32)).astype(BF)


def three(high, low, other_high, other_low, product):
    return product(high, other_high) + product(high, other_low) + product(low, other_high)


def kernel(
    panel_ref, slab_ref, cot_ref, inv_ref, upd_ref, gp_ref, gi_ref,
    strip, inv, inv_hi, inv_lo, k_hi, k_lo, perm, permt,
    graw, gs, sraw, pt, fn, tp, topt,
    q_sum, q_bf, n_own, n_send, e1, e2s, e2r, e3s, e3,
    r_bf, w, mst, d1, cmb, d2, wd, wc, wx, wy, wz, gpo, gio,
    ssem, rsem, lsem,
):
    row = lax.axis_index("row")
    col = lax.axis_index("col")
    y, z = row // 8, row % 8
    x, core = col // 2, col % 2
    twin = x * 2 + (1 - core)
    is_root = z == col
    mirror = y * 8 + col

    def x_at(d):
        return (x + d) % 4

    def col_at(d):
        return x_at(d) * 2 + core

    def row_y(d):
        return ((y + d) % 4) * 8 + z

    def row_z(d):
        return y * 8 + (z + d) % 8

    def remote(src, dst, send, recv, to_row, to_col):
        return pltpu.make_async_remote_copy(
            src_ref=src, dst_ref=dst, send_sem=ssem.at[send], recv_sem=rsem.at[recv],
            device_id=(to_row, to_col), device_id_type=MESH,
        )

    sent = []

    def send(src, dst, sem, to_row, to_col):
        copy = remote(src, dst, sem, sem, to_row, to_col)
        copy.start()
        sent.append(copy)

    def arrived(dst, sem):
        remote(dst, dst, sem, sem, row, twin).wait_recv()

    in_panel = pltpu.make_async_copy(panel_ref, strip, lsem.at[0])
    in_inv = pltpu.make_async_copy(inv_ref, inv, lsem.at[1])
    in_cot = pltpu.make_async_copy(cot_ref, graw, lsem.at[2])
    in_slab = pltpu.make_async_copy(slab_ref, sraw, lsem.at[3])
    in_panel.start()
    in_inv.start()
    in_cot.start()

    barrier = pltpu.get_barrier_semaphore()

    def hello(to_row, to_col):
        pl.semaphore_signal(barrier, inc=1, device_id=(to_row, to_col), device_id_type=MESH)

    hello(row, twin)
    for d in range(1, 4):
        hello(row, col_at(d))
        hello(row_y(d), col)
    for d in range(1, 8):
        hello(row_z(d), col)

    for d in range(1, 8):
        hello(mirror, (col + d) % 8)

    @pl.when(jnp.logical_not(is_root))
    def _():
        hello(mirror, col)

    in_panel.wait()
    for k in range(8):
        pt[k, col] = strip[k].astype(BF)

    r = lax.broadcasted_iota(jnp.int32, (256, 256), 0)
    q = lax.broadcasted_iota(jnp.int32, (256, 256), 1)
    perm[...] = jnp.where(q == (r % 64) * 4 + r // 64, 1.0, 0.0).astype(BF)
    permt[...] = jnp.where(r == (q % 64) * 4 + q // 64, 1.0, 0.0).astype(BF)
    in_inv.wait()
    high, low = halves(inv[...])
    inv_hi[...], inv_lo[...] = high, low
    t_high, t_low = halves(inv[...].T)
    k_hi[...], k_lo[...] = halves(three(t_high, t_low, high, low, nn))

    pl.semaphore_wait(barrier, 22 - is_root.astype(jnp.int32))

    def strip_to(d):
        return remote(pt.at[0, col], tp.at[y, col], S_B2 + d, S_B2 + col, row_z(d), z)

    for d in (1, 7, 2, 6, 3, 5, 4):
        strip_to(d).start()

    @pl.when(jnp.logical_not(is_root))
    def _():
        strip_to(0).start()

    @pl.when(is_root)
    def _():
        tp[y, z] = pt[0, col]

    def half(h, c):
        return pt.at[pl.ds(4 * h, 4), c]

    for h in range(2):
        for d in (1, 3, 2):
            send(half(h, col), half(h, col), S_A1 + 4 * h + d, row, col_at(d))
        send(half(h, col), half(h, col), S_A1 + 4 * h, row, twin)
    in_slab.start()

    def pass_on(h, d):
        origin = x_at(4 - d) * 2 + core
        arrived(half(h, origin), S_A1 + 4 * h + d)
        send(half(h, origin), half(h, origin), S_A2 + 4 * h + d, row, twin)

    def to_other_y(piece):
        for d in range(1, 4):
            remote(tp.at[y, piece], tp.at[y, piece], S_B3 + d, S_B3 + d, row_y(d), col).start()

    def piece_from(d):
        origin = (col + d) % 8
        if d == 0:

            @pl.when(jnp.logical_not(is_root))
            def _():
                arrived(tp.at[y, origin], S_B2 + origin)
        else:
            arrived(tp.at[y, origin], S_B2 + origin)
        to_other_y(origin)

    in_cot.wait()

    def split_columns(t, carry):
        block = graw[pl.ds(t * 64, 64)].reshape(256, 256)
        moved = nn(perm[...], block).astype(BF)
        for j in range(4):
            gs[pl.ds(t * 64, 64), j * 256 : (j + 1) * 256] = moved[j * 64 : (j + 1) * 64]
        return carry

    def split(t0, t1):
        lax.fori_loop(t0, t1, split_columns, 0, unroll=2)

    split(0, 8)
    piece_from(0)
    piece_from(1)
    piece_from(7)
    pass_on(0, 1)
    pass_on(0, 3)
    split(8, 12)
    piece_from(2)
    piece_from(6)
    pass_on(0, 2)
    split(12, 16)
    piece_from(3)
    piece_from(5)
    piece_from(4)
    split(16, 20)
    pass_on(1, 1)
    pass_on(1, 3)
    split(20, 26)
    pass_on(1, 2)
    split(26, 32)

    def panel_half(h):
        arrived(half(h, twin), S_A1 + 4 * h)
        for d in range(1, 4):
            origin = x_at(4 - d) * 2 + (1 - core)
            arrived(half(h, origin), S_A2 + 4 * h + d)

    def panel_rows(k0, k1):
        return jnp.concatenate([pt[k].reshape(256, 256) for k in range(k0, k1)], axis=1)

    panel_half(0)
    q_sum[...] = nn(panel_rows(0, 4), gs[0:1024, :])
    panel_half(1)

    def column_tile(j):
        columns = pl.ds(pl.multiple_of(j * 256, 256), 256)
        total = (q_sum[:, columns] + nn(panel_rows(4, 8), gs[1024:2048, columns])).astype(BF)
        q_bf[j] = total
        return nn(k_hi[...], total) + nn(k_lo[...], total)

    for d in (2, 1, 3):
        n_send[d] = column_tile((y + d) % 4).astype(BF)
        for h in range(2):
            rows = pl.ds(128 * h, 128)
            send(n_send.at[d, rows], e1.at[d, rows], S_E1 + 4 * h + d, row_y(d), col)
    n_own[...] = column_tile(y)

    for d in range(1, 4):
        arrived(tp.at[(y + 4 - d) % 4], S_B3 + d)

    def top_columns():
        return jnp.concatenate([tp[j].reshape(256, 256) for j in range(4)], axis=1)

    def column_sum(t, carry):
        rows = pl.ds(pl.multiple_of(t * 512, 512), 512)
        r_bf[rows, :] = nt(gs[rows, :], top_columns()).astype(BF)
        return carry

    lax.fori_loop(0, 4, column_sum, 0)
    q_all = jnp.concatenate([q_bf[j] for j in range(4)], axis=1)
    w[...] = (nn(panel_rows(0, 8), r_bf[...]) + nt(top_columns(), q_all)).reshape(4, 2, 32, 256)
    send(w.at[:, 1 - core], wd, S_WC, row, twin)

    def k_tile(k, carry):
        rows = pl.ds(pl.multiple_of(k * 256, 256), 256)
        value = nt(k_hi[...], r_bf[rows, :]) + nt(k_lo[...], r_bf[rows, :])
        mst[k] = value.reshape(4, 2, 32, 256).astype(BF)
        return carry

    def core_half(h):
        send(mst.at[pl.ds(4 * h, 4), :, 1 - core], d1.at[pl.ds(4 * h, 4)], S_D1 + h, row, twin)

    def join(h):
        arrived(d1.at[pl.ds(4 * h, 4)], S_D1 + h)
        for other in range(4):
            for k in range(4 * h, 4 * h + 4):
                cmb[other, k] = (mst[k, other, core].astype(F32) + d1[k, other].astype(F32)).astype(BF)
        for d in (1, 3, 2):
            part = pl.ds(4 * h, 4)
            send(cmb.at[x_at(d), part], d2.at[d, part], S_D2 + 4 * h + d, row, col_at(d))

    def strips_out(h):
        rows = pl.ds(128 * h, 128)
        total = n_own[rows, :]
        for d in range(1, 4):
            arrived(e1.at[d, rows], S_E1 + 4 * h + d)
            total += e1[d, rows, :].astype(F32)
        n_own[rows, :] = total
        e2s[pl.ds(4 * h, 4)] = total.reshape(4, 32, 256).astype(BF)
        for other in range(4 * h, 4 * h + 4):

            @pl.when(z != other)
            def _():
                remote(e2s.at[other], e2r.at[z], S_E2 + other, S_E2 + z, y * 8 + other, col).start()

    lax.fori_loop(0, 4, k_tile, 0)
    core_half(0)

    arrived(wd, S_WC)
    wc[...] = w[:, core] + wd[...]
    for d in (2, 1, 3):
        send(wc.at[x_at(d)], wx.at[d], S_WX + d, row, col_at(d))

    lax.fori_loop(4, 8, k_tile, 0)
    core_half(1)
    join(0)
    strips_out(0)
    join(1)
    strips_out(1)

    for d in range(1, 4):
        arrived(wx.at[d], S_WX + d)
    total = (wc[x] + wx[1] + wx[2] + wx[3]).astype(BF)
    wy[y] = total
    for d in (2, 1, 3):
        send(wy.at[y], wy.at[y], S_WY + d, row_y(d), col)

    def top_tile(j, carry):
        tile = tp[j].reshape(256, 256)
        topt[j] = (nn(inv_hi[...], tile) + nn(inv_lo[...], tile)).astype(BF)
        return carry

    def factor_tile(k, carry):
        tile = pt[k].reshape(256, 256)
        fn[k] = (nn(inv_hi[...], tile) + nn(inv_lo[...], tile)).T.astype(BF)
        return carry

    lax.fori_loop(0, 4, top_tile, 0)
    lax.fori_loop(0, 4, factor_tile, 0)

    for d in range(1, 4):
        arrived(wy.at[(y + 4 - d) % 4], S_WY + d)
    total = wy[0].astype(F32)
    for k in range(1, 4):
        total += wy[k].astype(F32)
    wz[z] = total.astype(BF)
    for d in (4, 3, 5, 2, 6, 1, 7):
        send(wz.at[z], wz.at[z], S_WZ + d, row_z(d), col)

    for d in range(1, 8):
        origin = (z + 8 - d) % 8
        arrived(e2r.at[origin], S_E2 + origin)
    e2r[z] = jnp.zeros((32, 256), BF)
    total = n_own[pl.ds(pl.multiple_of(z * 32, 32), 32), :]
    for k in range(8):
        total += e2r[k].astype(F32)
    e3s[...] = total.astype(BF)
    e3_out = remote(e3s, e3, S_E3, S_E3, mirror, z)

    @pl.when(jnp.logical_not(is_root))
    def _():
        e3_out.start()

    lax.fori_loop(4, 8, factor_tile, 0)
    in_slab.wait()

    def out_rows(k):
        rows = pl.ds(pl.multiple_of(k * 256, 256), 256)
        return pltpu.make_async_copy(sraw.at[rows], upd_ref.at[rows], lsem.at[4 + k])

    def update_tile(k, carry):
        start = pl.multiple_of(k * 256, 256)
        products = [nn(fn[k], topt[j]).astype(BF) for j in range(4)]
        for t in range(4):
            rows = pl.ds(pl.multiple_of(start + t * 64, 64), 64)
            product = jnp.concatenate([products[j][t * 64 : (t + 1) * 64] for j in range(4)], axis=0)
            old = sraw[rows].reshape(256, 256).astype(F32)
            sraw[rows] = (old - nn(permt[...], product)).astype(BF).reshape(64, 4, 256)
        out_rows(k).start()
        return carry

    lax.fori_loop(0, 8, update_tile, 0)

    for h in range(2):
        for d in range(1, 4):
            arrived(d2.at[d, pl.ds(4 * h, 4)], S_D2 + 4 * h + d)
    for k in range(1, 8):
        value = mst[k, x, core].astype(F32) + d1[k, x].astype(F32)
        for d in range(1, 4):
            value += d2[d, k].astype(F32)
        gpo[k] = -value

    @pl.when(is_root)
    def _():
        e3[...] = e3s[...]

    @pl.when(jnp.logical_not(is_root))
    def _():
        arrived(e3, S_E3)

    value = mst[0, x, core].astype(F32) + d1[0, x].astype(F32) + e3[...].astype(F32)
    for d in range(1, 4):
        value += d2[d, 0].astype(F32)
    gpo[0] = -value
    out_gp = pltpu.make_async_copy(gpo, gp_ref, lsem.at[12])
    out_gp.start()

    for d in range(1, 8):
        arrived(wz.at[(z + 8 - d) % 8], S_WZ + d)
    total = wz[0].astype(F32)
    for k in range(1, 8):
        total += wz[k].astype(F32)
    high, low = halves(total)
    gio[...] = -three(high, low, inv_hi[...], inv_lo[...], nt)
    out_gi = pltpu.make_async_copy(gio, gi_ref, lsem.at[13])
    out_gi.start()

    @pl.when(jnp.logical_not(is_root))
    def _():
        strip_to(0).wait_send()
        e3_out.wait_send()

    for d in range(1, 8):
        strip_to(d).wait_send()

    for d in range(1, 4):
        remote(tp.at[y], tp.at[y], S_B3 + d, S_B3 + d, row_y(d), col).wait_send()
    for other in range(8):

        @pl.when(z != other)
        def _():
            remote(e2s.at[other], e2r.at[z], S_E2 + other, S_E2 + z, y * 8 + other, col).wait_send()

    for copy in sent:
        copy.wait_send()
    for k in range(8):
        out_rows(k).wait()
    out_gp.wait()
    out_gi.wait()


def per_device(panel, slab, cotangent, inverse):
    strips = jnp.transpose(panel.reshape(8, 256, 32), (0, 2, 1))
    vmem = pltpu.VMEM
    updated, grad_panel, grad_inverse = pl.pallas_call(
        kernel,
        out_shape=(
            jax.ShapeDtypeStruct((2048, 4, 256), BF),
            jax.ShapeDtypeStruct((8, 32, 256), F32),
            jax.ShapeDtypeStruct((32, 256), F32),
        ),
        in_specs=[pl.BlockSpec(memory_space=pltpu.HBM)] * 4,
        out_specs=[pl.BlockSpec(memory_space=pl.ANY)] * 3,
        scratch_shapes=[
            vmem((8, 32, 256), F32), vmem((256, 256), F32),
            vmem((256, 256), BF), vmem((256, 256), BF), vmem((256, 256), BF), vmem((256, 256), BF),
            vmem((256, 256), BF), vmem((256, 256), BF),
            vmem((2048, 4, 256), BF), vmem((2048, 1024), BF), vmem((2048, 4, 256), BF),
            vmem((8, 8, 32, 256), BF), vmem((8, 256, 256), BF),
            vmem((4, 8, 32, 256), BF), vmem((4, 256, 256), BF),
            vmem((256, 1024), F32), vmem((4, 256, 256), BF), vmem((256, 256), F32),
            vmem((4, 256, 256), BF), vmem((4, 256, 256), BF),
            vmem((8, 32, 256), BF), vmem((8, 32, 256), BF),
            vmem((32, 256), BF), vmem((32, 256), BF),
            vmem((2048, 256), BF), vmem((4, 2, 32, 256), F32),
            vmem((8, 4, 2, 32, 256), BF), vmem((8, 4, 32, 256), BF),
            vmem((4, 8, 32, 256), BF), vmem((4, 8, 32, 256), BF),
            vmem((4, 32, 256), F32), vmem((4, 32, 256), F32), vmem((4, 32, 256), F32),
            vmem((4, 32, 256), BF), vmem((8, 32, 256), BF),
            vmem((8, 32, 256), F32), vmem((32, 256), F32),
            pltpu.SemaphoreType.DMA((N_SEM,)), pltpu.SemaphoreType.DMA((N_SEM,)), pltpu.SemaphoreType.DMA((14,)),
        ],
        compiler_params=pltpu.CompilerParams(
            collective_id=0, has_side_effects=True, vmem_limit_bytes=48 << 20
        ),
    )(strips, slab.reshape(2048, 4, 256), cotangent.reshape(2048, 4, 256), inverse)
    return (
        updated.reshape(slab.shape),
        jnp.transpose(grad_panel, (0, 2, 1)).reshape(panel.shape),
        jnp.transpose(grad_inverse),
    )


def solution(mesh):
    in_specs = (
        P(None, "row", None, "col"),
        P(None, "row", None, None, "col", None),
        P(None, "row", None, None, "col", None),
        P(),
    )
    out_specs = (
        P(None, "row", None, None, "col", None),
        P(None, "row", None, "col"),
        P(None, "col"),
    )
    return jax.shard_map(
        per_device, mesh=mesh, in_specs=in_specs, out_specs=out_specs, check_vma=False
    )
```

```python
import jax
import jax.numpy as jnp
from jax import lax
from jax.experimental import pallas as pl
from jax.experimental.pallas import tpu as pltpu
from jax.sharding import PartitionSpec as P

BF = jnp.bfloat16
F32 = jnp.float32
MESH = pl.DeviceIdType.MESH


S_A1, S_A2, S_B2, S_B3 = 0, 8, 17, 25
S_E1, S_E2, S_E3 = 29, 37, 45
S_D1, S_D2, S_WC, S_WX, S_WY, S_WZ = 46, 48, 56, 57, 61, 65
N_SEM = 73


def nn(a, b):
    return jnp.dot(a, b, preferred_element_type=F32)


def nt(a, b):
    return lax.dot_general(a, b, (((1,), (1,)), ((), ())), preferred_element_type=F32)


def halves(value):
    high = value.astype(BF)
    return high, (value - high.astype(F32)).astype(BF)


def three(high, low, other_high, other_low, product):
    return product(high, other_high) + product(high, other_low) + product(low, other_high)


def kernel(
    panel_ref, slab_ref, cot_ref, inv_ref, upd_ref, gp_ref, gi_ref,
    strip, inv, inv_hi, inv_lo, k_hi, k_lo, perm, permt,
    graw, gs, sraw, pt, fn, tp, topt,
    q_sum, q_bf, n_own, n_send, e1, e2s, e2r, e3s, e3,
    r_bf, w, mst, d1, cmb, d2, wd, wc, wx, wy, wz, gpo, gio,
    ssem, rsem, lsem,
):
    row = lax.axis_index("row")
    col = lax.axis_index("col")
    y, z = row // 8, row % 8
    x, core = col // 2, col % 2
    twin = x * 2 + (1 - core)
    is_root = z == col
    mirror = y * 8 + col

    def x_at(d):
        return (x + d) % 4

    def col_at(d):
        return x_at(d) * 2 + core

    def row_y(d):
        return ((y + d) % 4) * 8 + z

    def row_z(d):
        return y * 8 + (z + d) % 8

    def remote(src, dst, send, recv, to_row, to_col):
        return pltpu.make_async_remote_copy(
            src_ref=src, dst_ref=dst, send_sem=ssem.at[send], recv_sem=rsem.at[recv],
            device_id=(to_row, to_col), device_id_type=MESH,
        )

    sent = []

    def send(src, dst, sem, to_row, to_col):
        copy = remote(src, dst, sem, sem, to_row, to_col)
        copy.start()
        sent.append(copy)

    def arrived(dst, sem):
        remote(dst, dst, sem, sem, row, twin).wait_recv()

    in_panel = pltpu.make_async_copy(panel_ref, strip, lsem.at[0])
    in_inv = pltpu.make_async_copy(inv_ref, inv, lsem.at[1])
    in_cot = pltpu.make_async_copy(cot_ref, graw, lsem.at[2])
    in_slab = pltpu.make_async_copy(slab_ref, sraw, lsem.at[3])
    in_panel.start()
    in_inv.start()
    in_cot.start()

    barrier = pltpu.get_barrier_semaphore()

    def hello(to_row, to_col):
        pl.semaphore_signal(barrier, inc=1, device_id=(to_row, to_col), device_id_type=MESH)

    hello(row, twin)
    for d in range(1, 4):
        hello(row, col_at(d))
        hello(row_y(d), col)
    for d in range(1, 8):
        hello(row_z(d), col)

    for d in range(1, 8):
        hello(mirror, (col + d) % 8)

    @pl.when(jnp.logical_not(is_root))
    def _():
        hello(mirror, col)

    in_panel.wait()
    for k in range(8):
        pt[k, col] = strip[k].astype(BF)

    r = lax.broadcasted_iota(jnp.int32, (256, 256), 0)
    q = lax.broadcasted_iota(jnp.int32, (256, 256), 1)
    perm[...] = jnp.where(q == (r % 64) * 4 + r // 64, 1.0, 0.0).astype(BF)
    permt[...] = jnp.where(r == (q % 64) * 4 + q // 64, 1.0, 0.0).astype(BF)
    in_inv.wait()
    high, low = halves(inv[...])
    inv_hi[...], inv_lo[...] = high, low
    t_high, t_low = halves(inv[...].T)
    k_hi[...], k_lo[...] = halves(three(t_high, t_low, high, low, nn))

    pl.semaphore_wait(barrier, 22 - is_root.astype(jnp.int32))

    def strip_to(d):
        return remote(pt.at[0, col], tp.at[y, col], S_B2 + d, S_B2 + col, row_z(d), z)

    for d in (1, 7, 2, 6, 3, 5, 4):
        strip_to(d).start()

    @pl.when(jnp.logical_not(is_root))
    def _():
        strip_to(0).start()

    @pl.when(is_root)
    def _():
        tp[y, z] = pt[0, col]

    def half(h, c):
        return pt.at[pl.ds(4 * h, 4), c]

    for h in range(2):
        for d in (1, 3, 2):
            send(half(h, col), half(h, col), S_A1 + 4 * h + d, row, col_at(d))
        send(half(h, col), half(h, col), S_A1 + 4 * h, row, twin)
    in_slab.start()

    def pass_on(h, d):
        origin = x_at(4 - d) * 2 + core
        arrived(half(h, origin), S_A1 + 4 * h + d)
        send(half(h, origin), half(h, origin), S_A2 + 4 * h + d, row, twin)

    def to_other_y(piece):
        for d in range(1, 4):
            remote(tp.at[y, piece], tp.at[y, piece], S_B3 + d, S_B3 + d, row_y(d), col).start()

    def piece_from(d):
        origin = (col + d) % 8
        if d == 0:

            @pl.when(jnp.logical_not(is_root))
            def _():
                arrived(tp.at[y, origin], S_B2 + origin)
        else:
            arrived(tp.at[y, origin], S_B2 + origin)
        to_other_y(origin)

    in_cot.wait()

    def split_columns(t, carry):
        block = graw[pl.ds(t * 64, 64)].reshape(256, 256)
        moved = nn(perm[...], block).astype(BF)
        for j in range(4):
            gs[pl.ds(t * 64, 64), j * 256 : (j + 1) * 256] = moved[j * 64 : (j + 1) * 64]
        return carry

    def split(t0, t1):
        lax.fori_loop(t0, t1, split_columns, 0, unroll=2)

    split(0, 8)
    piece_from(0)
    piece_from(1)
    piece_from(7)
    pass_on(0, 1)
    pass_on(0, 3)
    split(8, 12)
    piece_from(2)
    piece_from(6)
    pass_on(0, 2)
    split(12, 16)
    piece_from(3)
    piece_from(5)
    piece_from(4)
    split(16, 20)
    pass_on(1, 1)
    pass_on(1, 3)
    split(20, 26)
    pass_on(1, 2)
    split(26, 32)

    def panel_half(h):
        arrived(half(h, twin), S_A1 + 4 * h)
        for d in range(1, 4):
            origin = x_at(4 - d) * 2 + (1 - core)
            arrived(half(h, origin), S_A2 + 4 * h + d)

    def panel_rows(k0, k1):
        return jnp.concatenate([pt[k].reshape(256, 256) for k in range(k0, k1)], axis=1)

    panel_half(0)
    q_sum[...] = nn(panel_rows(0, 4), gs[0:1024, :])
    panel_half(1)

    def column_tile(j):
        columns = pl.ds(pl.multiple_of(j * 256, 256), 256)
        total = (q_sum[:, columns] + nn(panel_rows(4, 8), gs[1024:2048, columns])).astype(BF)
        q_bf[j] = total
        return nn(k_hi[...], total) + nn(k_lo[...], total)

    def column_half(d, h):
        rows = pl.ds(128 * h, 128)
        send(n_send.at[d, rows], e1.at[d, rows], S_E1 + 4 * h + d, row_y(d), col)

    for d in (2, 1, 3):
        n_send[d] = column_tile((y + d) % 4).astype(BF)
        column_half(d, 0)
    for d in (2, 1, 3):
        column_half(d, 1)
    n_own[...] = column_tile(y)

    for d in range(1, 4):
        arrived(tp.at[(y + 4 - d) % 4], S_B3 + d)

    def top_columns():
        return jnp.concatenate([tp[j].reshape(256, 256) for j in range(4)], axis=1)

    def column_sum(t, carry):
        rows = pl.ds(pl.multiple_of(t * 512, 512), 512)
        r_bf[rows, :] = nt(gs[rows, :], top_columns()).astype(BF)
        return carry

    q_all = jnp.concatenate([q_bf[j] for j in range(4)], axis=1)
    w[...] = (nt(q_all, top_columns()) + nt(top_columns(), q_all)).reshape(4, 2, 32, 256)
    send(w.at[:, 1 - core], wd, S_WC, row, twin)
    lax.fori_loop(0, 4, column_sum, 0)

    def k_tile(k, carry):
        rows = pl.ds(pl.multiple_of(k * 256, 256), 256)
        value = nt(k_hi[...], r_bf[rows, :]) + nt(k_lo[...], r_bf[rows, :])
        mst[k] = value.reshape(4, 2, 32, 256).astype(BF)
        return carry

    def core_half(h):
        send(mst.at[pl.ds(4 * h, 4), :, 1 - core], d1.at[pl.ds(4 * h, 4)], S_D1 + h, row, twin)

    def join(h):
        arrived(d1.at[pl.ds(4 * h, 4)], S_D1 + h)
        for other in range(4):
            for k in range(4 * h, 4 * h + 4):
                cmb[other, k] = (mst[k, other, core].astype(F32) + d1[k, other].astype(F32)).astype(BF)
        for d in (1, 3, 2):
            part = pl.ds(4 * h, 4)
            send(cmb.at[x_at(d), part], d2.at[d, part], S_D2 + 4 * h + d, row, col_at(d))

    def strips_out(h):
        rows = pl.ds(128 * h, 128)
        total = n_own[rows, :]
        for d in range(1, 4):
            arrived(e1.at[d, rows], S_E1 + 4 * h + d)
            total += e1[d, rows, :].astype(F32)
        n_own[rows, :] = total
        e2s[pl.ds(4 * h, 4)] = total.reshape(4, 32, 256).astype(BF)
        for other in range(4 * h, 4 * h + 4):

            @pl.when(z != other)
            def _():
                remote(e2s.at[other], e2r.at[z], S_E2 + other, S_E2 + z, y * 8 + other, col).start()

    arrived(wd, S_WC)
    wc[...] = w[:, core] + wd[...]
    for d in (2, 1, 3):
        send(wc.at[x_at(d)], wx.at[d], S_WX + d, row, col_at(d))

    lax.fori_loop(0, 4, k_tile, 0)
    core_half(0)
    strips_out(0)
    lax.fori_loop(4, 8, k_tile, 0)
    core_half(1)
    join(0)
    strips_out(1)

    for d in range(1, 4):
        arrived(wx.at[d], S_WX + d)
    total = (wc[x] + wx[1] + wx[2] + wx[3]).astype(BF)
    wy[y] = total
    for d in (2, 1, 3):
        send(wy.at[y], wy.at[y], S_WY + d, row_y(d), col)
    join(1)

    def top_tile(j, carry):
        tile = tp[j].reshape(256, 256)
        topt[j] = (nn(inv_hi[...], tile) + nn(inv_lo[...], tile)).astype(BF)
        return carry

    def factor_tile(k, carry):
        tile = pt[k].reshape(256, 256)
        fn[k] = (nn(inv_hi[...], tile) + nn(inv_lo[...], tile)).T.astype(BF)
        return carry

    lax.fori_loop(0, 4, top_tile, 0)
    lax.fori_loop(0, 8, factor_tile, 0)

    for d in range(1, 4):
        arrived(wy.at[(y + 4 - d) % 4], S_WY + d)
    total = wy[0].astype(F32)
    for k in range(1, 4):
        total += wy[k].astype(F32)
    wz[z] = total.astype(BF)
    for d in (4, 3, 5, 2, 6, 1, 7):
        send(wz.at[z], wz.at[z], S_WZ + d, row_z(d), col)

    for d in range(1, 8):
        origin = (z + 8 - d) % 8
        arrived(e2r.at[origin], S_E2 + origin)
    e2r[z] = jnp.zeros((32, 256), BF)
    total = n_own[pl.ds(pl.multiple_of(z * 32, 32), 32), :]
    for k in range(8):
        total += e2r[k].astype(F32)
    e3s[...] = total.astype(BF)
    e3_out = remote(e3s, e3, S_E3, S_E3, mirror, z)

    @pl.when(jnp.logical_not(is_root))
    def _():
        e3_out.start()

    in_slab.wait()

    def out_rows(k):
        rows = pl.ds(pl.multiple_of(k * 256, 256), 256)
        return pltpu.make_async_copy(sraw.at[rows], upd_ref.at[rows], lsem.at[4 + k])

    def update_tile(k, carry):
        start = pl.multiple_of(k * 256, 256)
        products = [nn(fn[k], topt[j]).astype(BF) for j in range(4)]
        for t in range(4):
            rows = pl.ds(pl.multiple_of(start + t * 64, 64), 64)
            product = jnp.concatenate([products[j][t * 64 : (t + 1) * 64] for j in range(4)], axis=0)
            old = sraw[rows].reshape(256, 256).astype(F32)
            sraw[rows] = (old - nn(permt[...], product)).astype(BF).reshape(64, 4, 256)
        out_rows(k).start()
        return carry

    lax.fori_loop(0, 8, update_tile, 0)

    for h in range(2):
        for d in range(1, 4):
            arrived(d2.at[d, pl.ds(4 * h, 4)], S_D2 + 4 * h + d)
    for k in range(1, 8):
        value = mst[k, x, core].astype(F32) + d1[k, x].astype(F32)
        for d in range(1, 4):
            value += d2[d, k].astype(F32)
        gpo[k] = -value

    @pl.when(is_root)
    def _():
        e3[...] = e3s[...]

    @pl.when(jnp.logical_not(is_root))
    def _():
        arrived(e3, S_E3)

    value = mst[0, x, core].astype(F32) + d1[0, x].astype(F32) + e3[...].astype(F32)
    for d in range(1, 4):
        value += d2[d, 0].astype(F32)
    gpo[0] = -value
    out_gp = pltpu.make_async_copy(gpo, gp_ref, lsem.at[12])
    out_gp.start()

    for d in range(1, 8):
        arrived(wz.at[(z + 8 - d) % 8], S_WZ + d)
    total = wz[0].astype(F32)
    for k in range(1, 8):
        total += wz[k].astype(F32)
    high, low = halves(total)
    gio[...] = -three(high, low, inv_hi[...], inv_lo[...], nt)
    out_gi = pltpu.make_async_copy(gio, gi_ref, lsem.at[13])
    out_gi.start()

    @pl.when(jnp.logical_not(is_root))
    def _():
        strip_to(0).wait_send()
        e3_out.wait_send()

    for d in range(1, 8):
        strip_to(d).wait_send()

    for d in range(1, 4):
        remote(tp.at[y], tp.at[y], S_B3 + d, S_B3 + d, row_y(d), col).wait_send()
    for other in range(8):

        @pl.when(z != other)
        def _():
            remote(e2s.at[other], e2r.at[z], S_E2 + other, S_E2 + z, y * 8 + other, col).wait_send()

    for copy in sent:
        copy.wait_send()
    for k in range(8):
        out_rows(k).wait()
    out_gp.wait()
    out_gi.wait()


def per_device(panel, slab, cotangent, inverse):
    strips = jnp.transpose(panel.reshape(8, 256, 32), (0, 2, 1))
    vmem = pltpu.VMEM
    updated, grad_panel, grad_inverse = pl.pallas_call(
        kernel,
        out_shape=(
            jax.ShapeDtypeStruct((2048, 4, 256), BF),
            jax.ShapeDtypeStruct((8, 32, 256), F32),
            jax.ShapeDtypeStruct((32, 256), F32),
        ),
        in_specs=[pl.BlockSpec(memory_space=pltpu.HBM)] * 4,
        out_specs=[pl.BlockSpec(memory_space=pl.ANY)] * 3,
        scratch_shapes=[
            vmem((8, 32, 256), F32), vmem((256, 256), F32),
            vmem((256, 256), BF), vmem((256, 256), BF), vmem((256, 256), BF), vmem((256, 256), BF),
            vmem((256, 256), BF), vmem((256, 256), BF),
            vmem((2048, 4, 256), BF), vmem((2048, 1024), BF), vmem((2048, 4, 256), BF),
            vmem((8, 8, 32, 256), BF), vmem((8, 256, 256), BF),
            vmem((4, 8, 32, 256), BF), vmem((4, 256, 256), BF),
            vmem((256, 1024), F32), vmem((4, 256, 256), BF), vmem((256, 256), F32),
            vmem((4, 256, 256), BF), vmem((4, 256, 256), BF),
            vmem((8, 32, 256), BF), vmem((8, 32, 256), BF),
            vmem((32, 256), BF), vmem((32, 256), BF),
            vmem((2048, 256), BF), vmem((4, 2, 32, 256), F32),
            vmem((8, 4, 2, 32, 256), BF), vmem((8, 4, 32, 256), BF),
            vmem((4, 8, 32, 256), BF), vmem((4, 8, 32, 256), BF),
            vmem((4, 32, 256), F32), vmem((4, 32, 256), F32), vmem((4, 32, 256), F32),
            vmem((4, 32, 256), BF), vmem((8, 32, 256), BF),
            vmem((8, 32, 256), F32), vmem((32, 256), F32),
            pltpu.SemaphoreType.DMA((N_SEM,)), pltpu.SemaphoreType.DMA((N_SEM,)), pltpu.SemaphoreType.DMA((14,)),
        ],
        compiler_params=pltpu.CompilerParams(
            collective_id=0, has_side_effects=True, vmem_limit_bytes=48 << 20
        ),
    )(pltpu.with_memory_space_constraint(strips, pltpu.HBM), slab.reshape(2048, 4, 256), cotangent.reshape(2048, 4, 256), pltpu.with_memory_space_constraint(inverse, pltpu.HBM))
    return (
        updated.reshape(slab.shape),
        jnp.transpose(grad_panel, (0, 2, 1)).reshape(panel.shape),
        jnp.transpose(grad_inverse),
    )


def solution(mesh):
    in_specs = (
        P(None, "row", None, "col"),
        P(None, "row", None, None, "col", None),
        P(None, "row", None, None, "col", None),
        P(),
    )
    out_specs = (
        P(None, "row", None, None, "col", None),
        P(None, "row", None, "col"),
        P(None, "col"),
    )
    return jax.shard_map(
        per_device, mesh=mesh, in_specs=in_specs, out_specs=out_specs, check_vma=False
    )
```

```python
import jax
import jax.numpy as jnp
from jax import lax
from jax.experimental import pallas as pl
from jax.experimental.pallas import tpu as pltpu
from jax.sharding import PartitionSpec as P

BF = jnp.bfloat16
F32 = jnp.float32
MESH = pl.DeviceIdType.MESH


S_A1, S_A2, S_B2, S_B3 = 0, 8, 17, 25
S_E1, S_E2 = 29, 37
S_D1, S_D2, S_WC, S_WX, S_WY, S_WZ = 46, 48, 56, 57, 61, 65
N_SEM = 73


def nn(a, b):
    return jnp.dot(a, b, preferred_element_type=F32)


def nt(a, b):
    return lax.dot_general(a, b, (((1,), (1,)), ((), ())), preferred_element_type=F32)


def halves(value):
    high = value.astype(BF)
    return high, (value - high.astype(F32)).astype(BF)


def three(high, low, other_high, other_low, product):
    return product(high, other_high) + product(high, other_low) + product(low, other_high)


def kernel(
    panel_ref, slab_ref, cot_ref, inv_ref, upd_ref, gp_ref, gi_ref,
    strip, inv, inv_hi, inv_lo, k_hi, k_lo, perm, permt,
    graw, gs, sraw, pt, fn, tp, topt,
    q_sum, q_bf, n_own, n_send, e1, e2s, e2r,
    r_bf, w, mst, d1, cmb, d2, wd, wc, wx, wy, wz, gpo, gio,
    ssem, rsem, lsem,
):
    row = lax.axis_index("row")
    col = lax.axis_index("col")
    y, z = row // 8, row % 8
    x, core = col // 2, col % 2
    twin = x * 2 + (1 - core)
    is_root = z == col
    mirror = y * 8 + col

    def x_at(d):
        return (x + d) % 4

    def col_at(d):
        return x_at(d) * 2 + core

    def row_y(d):
        return ((y + d) % 4) * 8 + z

    def row_z(d):
        return y * 8 + (z + d) % 8

    def remote(src, dst, send, recv, to_row, to_col):
        return pltpu.make_async_remote_copy(
            src_ref=src, dst_ref=dst, send_sem=ssem.at[send], recv_sem=rsem.at[recv],
            device_id=(to_row, to_col), device_id_type=MESH,
        )

    sent = []

    def send(src, dst, sem, to_row, to_col):
        copy = remote(src, dst, sem, sem, to_row, to_col)
        copy.start()
        sent.append(copy)

    def arrived(dst, sem):
        remote(dst, dst, sem, sem, row, twin).wait_recv()

    in_panel = pltpu.make_async_copy(panel_ref, strip, lsem.at[0])
    in_inv = pltpu.make_async_copy(inv_ref, inv, lsem.at[1])
    in_cot = pltpu.make_async_copy(cot_ref, graw, lsem.at[2])
    in_slab = pltpu.make_async_copy(slab_ref, sraw, lsem.at[3])
    in_panel.start()
    in_inv.start()
    in_cot.start()

    barrier = pltpu.get_barrier_semaphore()

    def hello(to_row, to_col):
        pl.semaphore_signal(barrier, inc=1, device_id=(to_row, to_col), device_id_type=MESH)

    hello(row, twin)
    for d in range(1, 4):
        hello(row, col_at(d))
        hello(row_y(d), col)
    for d in range(1, 8):
        hello(row_z(d), col)

    for d in range(1, 8):
        hello(mirror, (col + d) % 8)

    @pl.when(jnp.logical_not(is_root))
    def _():
        hello(mirror, col)

    in_panel.wait()
    for k in range(8):
        pt[k, col] = strip[k].astype(BF)

    r = lax.broadcasted_iota(jnp.int32, (256, 256), 0)
    q = lax.broadcasted_iota(jnp.int32, (256, 256), 1)
    perm[...] = jnp.where(q == (r % 64) * 4 + r // 64, 1.0, 0.0).astype(BF)
    permt[...] = jnp.where(r == (q % 64) * 4 + q // 64, 1.0, 0.0).astype(BF)
    in_inv.wait()
    high, low = halves(inv[...])
    inv_hi[...], inv_lo[...] = high, low
    t_high, t_low = halves(inv[...].T)
    k_hi[...], k_lo[...] = halves(three(t_high, t_low, high, low, nn))

    pl.semaphore_wait(barrier, 22 - is_root.astype(jnp.int32))

    def strip_to(d):
        return remote(pt.at[0, col], tp.at[y, col], S_B2 + d, S_B2 + col, row_z(d), z)

    for d in (1, 7, 2, 6, 3, 5, 4):
        strip_to(d).start()

    @pl.when(jnp.logical_not(is_root))
    def _():
        strip_to(0).start()

    @pl.when(is_root)
    def _():
        tp[y, z] = pt[0, col]

    def half(h, c):
        return pt.at[pl.ds(4 * h, 4), c]

    for h in range(2):
        for d in (1, 3, 2):
            send(half(h, col), half(h, col), S_A1 + 4 * h + d, row, col_at(d))
        send(half(h, col), half(h, col), S_A1 + 4 * h, row, twin)
    in_slab.start()

    def pass_on(h, d):
        origin = x_at(4 - d) * 2 + core
        arrived(half(h, origin), S_A1 + 4 * h + d)
        send(half(h, origin), half(h, origin), S_A2 + 4 * h + d, row, twin)

    def to_other_y(piece):
        for d in range(1, 4):
            remote(tp.at[y, piece], tp.at[y, piece], S_B3 + d, S_B3 + d, row_y(d), col).start()

    def piece_from(d):
        origin = (col + d) % 8
        if d == 0:

            @pl.when(jnp.logical_not(is_root))
            def _():
                arrived(tp.at[y, origin], S_B2 + origin)
        else:
            arrived(tp.at[y, origin], S_B2 + origin)
        to_other_y(origin)

    in_cot.wait()

    def split_columns(t, carry):
        block = graw[pl.ds(t * 64, 64)].reshape(256, 256)
        moved = nn(perm[...], block).astype(BF)
        for j in range(4):
            gs[pl.ds(t * 64, 64), j * 256 : (j + 1) * 256] = moved[j * 64 : (j + 1) * 64]
        return carry

    def split(t0, t1):
        lax.fori_loop(t0, t1, split_columns, 0, unroll=2)

    split(0, 8)
    piece_from(0)
    piece_from(1)
    piece_from(7)
    pass_on(0, 1)
    pass_on(0, 3)
    split(8, 12)
    piece_from(2)
    piece_from(6)
    pass_on(0, 2)
    split(12, 16)
    piece_from(3)
    piece_from(5)
    piece_from(4)
    split(16, 20)
    pass_on(1, 1)
    pass_on(1, 3)
    split(20, 26)
    pass_on(1, 2)
    split(26, 32)

    def panel_half(h):
        arrived(half(h, twin), S_A1 + 4 * h)
        for d in range(1, 4):
            origin = x_at(4 - d) * 2 + (1 - core)
            arrived(half(h, origin), S_A2 + 4 * h + d)

    def panel_rows(k0, k1):
        return jnp.concatenate([pt[k].reshape(256, 256) for k in range(k0, k1)], axis=1)

    panel_half(0)
    q_sum[...] = nn(panel_rows(0, 4), gs[0:1024, :])
    panel_half(1)

    def column_tile(j):
        columns = pl.ds(pl.multiple_of(j * 256, 256), 256)
        total = (q_sum[:, columns] + nn(panel_rows(4, 8), gs[1024:2048, columns])).astype(BF)
        q_bf[j] = total
        return nn(k_hi[...], total) + nn(k_lo[...], total)

    def column_half(d, h):
        rows = pl.ds(128 * h, 128)
        send(n_send.at[d, rows], e1.at[d, rows], S_E1 + 4 * h + d, row_y(d), col)

    for d in (2, 1, 3):
        n_send[d] = column_tile((y + d) % 4).astype(BF)
        column_half(d, 0)
    for d in (2, 1, 3):
        column_half(d, 1)
    n_own[...] = column_tile(y)

    for d in range(1, 4):
        arrived(tp.at[(y + 4 - d) % 4], S_B3 + d)

    def top_columns():
        return jnp.concatenate([tp[j].reshape(256, 256) for j in range(4)], axis=1)

    def column_sum(t, carry):
        rows = pl.ds(pl.multiple_of(t * 512, 512), 512)
        r_bf[rows, :] = nt(gs[rows, :], top_columns()).astype(BF)
        return carry

    q_all = jnp.concatenate([q_bf[j] for j in range(4)], axis=1)
    w[...] = (nt(q_all, top_columns()) + nt(top_columns(), q_all)).reshape(4, 2, 32, 256)
    send(w.at[:, 1 - core], wd, S_WC, row, twin)
    lax.fori_loop(0, 4, column_sum, 0)

    def k_tile(k, carry):
        rows = pl.ds(pl.multiple_of(k * 256, 256), 256)
        value = nt(k_hi[...], r_bf[rows, :]) + nt(k_lo[...], r_bf[rows, :])
        mst[k] = value.reshape(4, 2, 32, 256).astype(BF)
        return carry

    def core_half(h):
        send(mst.at[pl.ds(4 * h, 4), :, 1 - core], d1.at[pl.ds(4 * h, 4)], S_D1 + h, row, twin)

    def join(h):
        arrived(d1.at[pl.ds(4 * h, 4)], S_D1 + h)
        for other in range(4):
            for k in range(4 * h, 4 * h + 4):
                cmb[other, k] = (mst[k, other, core].astype(F32) + d1[k, other].astype(F32)).astype(BF)
        for d in (1, 3, 2):
            part = pl.ds(4 * h, 4)
            send(cmb.at[x_at(d), part], d2.at[d, part], S_D2 + 4 * h + d, row, col_at(d))

    def strip_home(other):
        return remote(e2s.at[other], e2r.at[z], S_E2 + other, S_E2 + z, mirror, other)

    def leaves(other):
        return jnp.logical_or(z != col, col != other)

    def strips_out(h):
        rows = pl.ds(128 * h, 128)
        total = n_own[rows, :]
        for d in range(1, 4):
            arrived(e1.at[d, rows], S_E1 + 4 * h + d)
            total += e1[d, rows, :].astype(F32)
        e2s[pl.ds(4 * h, 4)] = total.reshape(4, 32, 256).astype(BF)
        for other in range(4 * h, 4 * h + 4):

            @pl.when(leaves(other))
            def _():
                strip_home(other).start()

    arrived(wd, S_WC)
    wc[...] = w[:, core] + wd[...]
    for d in (2, 1, 3):
        send(wc.at[x_at(d)], wx.at[d], S_WX + d, row, col_at(d))

    lax.fori_loop(0, 4, k_tile, 0)
    core_half(0)
    lax.fori_loop(4, 8, k_tile, 0)
    core_half(1)
    join(0)
    strips_out(0)
    for d in range(1, 4):
        arrived(wx.at[d], S_WX + d)
    total = (wc[x] + wx[1] + wx[2] + wx[3]).astype(BF)
    wy[y] = total
    for d in (2, 1, 3):
        send(wy.at[y], wy.at[y], S_WY + d, row_y(d), col)
    strips_out(1)
    join(1)

    def top_tile(j, carry):
        tile = tp[j].reshape(256, 256)
        topt[j] = (nn(inv_hi[...], tile) + nn(inv_lo[...], tile)).astype(BF)
        return carry

    def factor_tile(k, carry):
        tile = pt[k].reshape(256, 256)
        fn[k] = (nn(inv_hi[...], tile) + nn(inv_lo[...], tile)).T.astype(BF)
        return carry

    lax.fori_loop(0, 4, top_tile, 0)
    lax.fori_loop(0, 8, factor_tile, 0)

    for d in range(1, 4):
        arrived(wy.at[(y + 4 - d) % 4], S_WY + d)
    total = wy[0].astype(F32)
    for k in range(1, 4):
        total += wy[k].astype(F32)
    wz[z] = total.astype(BF)
    for d in (4, 3, 5, 2, 6, 1, 7):
        send(wz.at[z], wz.at[z], S_WZ + d, row_z(d), col)

    in_slab.wait()

    def out_rows(k):
        rows = pl.ds(pl.multiple_of(k * 256, 256), 256)
        return pltpu.make_async_copy(sraw.at[rows], upd_ref.at[rows], lsem.at[4 + k])

    def update_tile(k, carry):
        start = pl.multiple_of(k * 256, 256)
        products = [nn(fn[k], topt[j]).astype(BF) for j in range(4)]
        for t in range(4):
            rows = pl.ds(pl.multiple_of(start + t * 64, 64), 64)
            product = jnp.concatenate([products[j][t * 64 : (t + 1) * 64] for j in range(4)], axis=0)
            old = sraw[rows].reshape(256, 256).astype(F32)
            sraw[rows] = (old - nn(permt[...], product)).astype(BF).reshape(64, 4, 256)
        out_rows(k).start()
        return carry

    lax.fori_loop(0, 8, update_tile, 0)

    for h in range(2):
        for d in range(1, 4):
            arrived(d2.at[d, pl.ds(4 * h, 4)], S_D2 + 4 * h + d)
    for k in range(1, 8):
        value = mst[k, x, core].astype(F32) + d1[k, x].astype(F32)
        for d in range(1, 4):
            value += d2[d, k].astype(F32)
        gpo[k] = -value

    for d in range(1, 8):
        origin = (z + d) % 8
        arrived(e2r.at[origin], S_E2 + origin)

    @pl.when(is_root)
    def _():
        e2r[z] = e2s[col]

    @pl.when(jnp.logical_not(is_root))
    def _():
        arrived(e2r.at[z], S_E2 + z)

    value = mst[0, x, core].astype(F32) + d1[0, x].astype(F32)
    for origin in range(8):
        value += e2r[origin].astype(F32)
    for d in range(1, 4):
        value += d2[d, 0].astype(F32)
    gpo[0] = -value
    out_gp = pltpu.make_async_copy(gpo, gp_ref, lsem.at[12])
    out_gp.start()

    for d in range(1, 8):
        arrived(wz.at[(z + 8 - d) % 8], S_WZ + d)
    total = wz[0].astype(F32)
    for k in range(1, 8):
        total += wz[k].astype(F32)
    high, low = halves(total)
    gio[...] = -three(high, low, inv_hi[...], inv_lo[...], nt)
    out_gi = pltpu.make_async_copy(gio, gi_ref, lsem.at[13])
    out_gi.start()

    @pl.when(jnp.logical_not(is_root))
    def _():
        strip_to(0).wait_send()

    for d in range(1, 8):
        strip_to(d).wait_send()

    for d in range(1, 4):
        remote(tp.at[y], tp.at[y], S_B3 + d, S_B3 + d, row_y(d), col).wait_send()
    for other in range(8):

        @pl.when(leaves(other))
        def _():
            strip_home(other).wait_send()

    for copy in sent:
        copy.wait_send()
    for k in range(8):
        out_rows(k).wait()
    out_gp.wait()
    out_gi.wait()


def per_device(panel, slab, cotangent, inverse):
    strips = jnp.transpose(panel.reshape(8, 256, 32), (0, 2, 1))
    vmem = pltpu.VMEM
    updated, grad_panel, grad_inverse = pl.pallas_call(
        kernel,
        out_shape=(
            jax.ShapeDtypeStruct((2048, 4, 256), BF),
            jax.ShapeDtypeStruct((8, 32, 256), F32),
            jax.ShapeDtypeStruct((32, 256), F32),
        ),
        in_specs=[pl.BlockSpec(memory_space=pltpu.HBM)] * 4,
        out_specs=[pl.BlockSpec(memory_space=pl.ANY)] * 3,
        scratch_shapes=[
            vmem((8, 32, 256), F32), vmem((256, 256), F32),
            vmem((256, 256), BF), vmem((256, 256), BF), vmem((256, 256), BF), vmem((256, 256), BF),
            vmem((256, 256), BF), vmem((256, 256), BF),
            vmem((2048, 4, 256), BF), vmem((2048, 1024), BF), vmem((2048, 4, 256), BF),
            vmem((8, 8, 32, 256), BF), vmem((8, 256, 256), BF),
            vmem((4, 8, 32, 256), BF), vmem((4, 256, 256), BF),
            vmem((256, 1024), F32), vmem((4, 256, 256), BF), vmem((256, 256), F32),
            vmem((4, 256, 256), BF), vmem((4, 256, 256), BF),
            vmem((8, 32, 256), BF), vmem((8, 32, 256), BF),
            vmem((2048, 256), BF), vmem((4, 2, 32, 256), F32),
            vmem((8, 4, 2, 32, 256), BF), vmem((8, 4, 32, 256), BF),
            vmem((4, 8, 32, 256), BF), vmem((4, 8, 32, 256), BF),
            vmem((4, 32, 256), F32), vmem((4, 32, 256), F32), vmem((4, 32, 256), F32),
            vmem((4, 32, 256), BF), vmem((8, 32, 256), BF),
            vmem((8, 32, 256), F32), vmem((32, 256), F32),
            pltpu.SemaphoreType.DMA((N_SEM,)), pltpu.SemaphoreType.DMA((N_SEM,)), pltpu.SemaphoreType.DMA((14,)),
        ],
        compiler_params=pltpu.CompilerParams(
            collective_id=0, has_side_effects=True, vmem_limit_bytes=48 << 20
        ),
    )(pltpu.with_memory_space_constraint(strips, pltpu.HBM), slab.reshape(2048, 4, 256), cotangent.reshape(2048, 4, 256), pltpu.with_memory_space_constraint(inverse, pltpu.HBM))
    return (
        updated.reshape(slab.shape),
        jnp.transpose(grad_panel, (0, 2, 1)).reshape(panel.shape),
        jnp.transpose(grad_inverse),
    )


def solution(mesh):
    in_specs = (
        P(None, "row", None, "col"),
        P(None, "row", None, None, "col", None),
        P(None, "row", None, None, "col", None),
        P(),
    )
    out_specs = (
        P(None, "row", None, None, "col", None),
        P(None, "row", None, "col"),
        P(None, "col"),
    )
    return jax.shard_map(
        per_device, mesh=mesh, in_specs=in_specs, out_specs=out_specs, check_vma=False
    )
```

```python
import jax
import jax.numpy as jnp
from jax import lax
from jax.experimental import pallas as pl
from jax.experimental.pallas import tpu as pltpu
from jax.sharding import PartitionSpec as P

BF = jnp.bfloat16
F32 = jnp.float32
MESH = pl.DeviceIdType.MESH


S_A1, S_A2, S_B2, S_B3 = 0, 8, 17, 25
S_E1, S_E2, S_E3 = 29, 37, 45
S_D1, S_D2, S_WC, S_WX, S_WY, S_WZ = 46, 48, 56, 57, 61, 65
N_SEM = 73


def nn(a, b):
    return jnp.dot(a, b, preferred_element_type=F32)


def nt(a, b):
    return lax.dot_general(a, b, (((1,), (1,)), ((), ())), preferred_element_type=F32)


def halves(value):
    high = value.astype(BF)
    return high, (value - high.astype(F32)).astype(BF)


def three(high, low, other_high, other_low, product):
    return product(high, other_high) + product(high, other_low) + product(low, other_high)


def kernel(
    panel_ref, slab_ref, cot_ref, inv_ref, upd_ref, gp_ref, gi_ref,
    strip, inv, inv_hi, inv_lo, k_hi, k_lo, perm, permt,
    graw, gs, sraw, pt, fn, tp, topt,
    q_sum, q_bf, n_own, n_send, e1, e2s, e2r, e3s, e3,
    r_bf, w, mst, d1, cmb, d2, wd, wc, wx, wy, wz, gpo, gio,
    ssem, rsem, lsem,
):
    row = lax.axis_index("row")
    col = lax.axis_index("col")
    y, z = row // 8, row % 8
    x, core = col // 2, col % 2
    twin = x * 2 + (1 - core)
    is_root = z == col
    mirror = y * 8 + col

    def x_at(d):
        return (x + d) % 4

    def col_at(d):
        return x_at(d) * 2 + core

    def row_y(d):
        return ((y + d) % 4) * 8 + z

    def row_z(d):
        return y * 8 + (z + d) % 8

    def remote(src, dst, send, recv, to_row, to_col):
        return pltpu.make_async_remote_copy(
            src_ref=src, dst_ref=dst, send_sem=ssem.at[send], recv_sem=rsem.at[recv],
            device_id=(to_row, to_col), device_id_type=MESH,
        )

    sent = []

    def send(src, dst, sem, to_row, to_col):
        copy = remote(src, dst, sem, sem, to_row, to_col)
        copy.start()
        sent.append(copy)

    def arrived(dst, sem):
        remote(dst, dst, sem, sem, row, twin).wait_recv()

    in_panel = pltpu.make_async_copy(panel_ref, strip, lsem.at[0])
    in_inv = pltpu.make_async_copy(inv_ref, inv, lsem.at[1])
    in_cot = pltpu.make_async_copy(cot_ref, graw, lsem.at[2])
    in_slab = pltpu.make_async_copy(slab_ref, sraw, lsem.at[3])
    in_panel.start()
    in_inv.start()
    in_cot.start()

    barrier = pltpu.get_barrier_semaphore()

    def hello(to_row, to_col):
        pl.semaphore_signal(barrier, inc=1, device_id=(to_row, to_col), device_id_type=MESH)

    hello(row, twin)
    for d in range(1, 4):
        hello(row, col_at(d))
        hello(row_y(d), col)
    for d in range(1, 8):
        hello(row_z(d), col)

    for d in range(1, 8):
        hello(mirror, (col + d) % 8)

    @pl.when(jnp.logical_not(is_root))
    def _():
        hello(mirror, col)

    in_panel.wait()
    for k in range(8):
        pt[k, col] = strip[k].astype(BF)

    r = lax.broadcasted_iota(jnp.int32, (256, 256), 0)
    q = lax.broadcasted_iota(jnp.int32, (256, 256), 1)
    perm[...] = jnp.where(q == (r % 64) * 4 + r // 64, 1.0, 0.0).astype(BF)
    permt[...] = jnp.where(r == (q % 64) * 4 + q // 64, 1.0, 0.0).astype(BF)
    in_inv.wait()
    high, low = halves(inv[...])
    inv_hi[...], inv_lo[...] = high, low
    t_high, t_low = halves(inv[...].T)
    k_hi[...], k_lo[...] = halves(three(t_high, t_low, high, low, nn))

    pl.semaphore_wait(barrier, 22 - is_root.astype(jnp.int32))

    def strip_to(d):
        return remote(pt.at[0, col], tp.at[y, col], S_B2 + d, S_B2 + col, row_z(d), z)

    for d in (1, 7, 2, 6, 3, 5, 4):
        strip_to(d).start()

    @pl.when(jnp.logical_not(is_root))
    def _():
        strip_to(0).start()

    @pl.when(is_root)
    def _():
        tp[y, z] = pt[0, col]

    def half(h, c):
        return pt.at[pl.ds(4 * h, 4), c]

    for h in range(2):
        for d in (1, 3, 2):
            send(half(h, col), half(h, col), S_A1 + 4 * h + d, row, col_at(d))
        send(half(h, col), half(h, col), S_A1 + 4 * h, row, twin)
    in_slab.start()

    def pass_on(h, d):
        origin = x_at(4 - d) * 2 + core
        arrived(half(h, origin), S_A1 + 4 * h + d)
        send(half(h, origin), half(h, origin), S_A2 + 4 * h + d, row, twin)

    def to_other_y(piece):
        for d in range(1, 4):
            remote(tp.at[y, piece], tp.at[y, piece], S_B3 + d, S_B3 + d, row_y(d), col).start()

    def piece_from(d):
        origin = (col + d) % 8
        if d == 0:

            @pl.when(jnp.logical_not(is_root))
            def _():
                arrived(tp.at[y, origin], S_B2 + origin)
        else:
            arrived(tp.at[y, origin], S_B2 + origin)
        to_other_y(origin)

    in_cot.wait()

    def split_columns(t, carry):
        block = graw[pl.ds(t * 64, 64)].reshape(256, 256)
        moved = nn(perm[...], block).astype(BF)
        for j in range(4):
            gs[pl.ds(t * 64, 64), j * 256 : (j + 1) * 256] = moved[j * 64 : (j + 1) * 64]
        return carry

    def split(t0, t1):
        lax.fori_loop(t0, t1, split_columns, 0, unroll=2)

    split(0, 8)
    piece_from(0)
    piece_from(1)
    piece_from(7)
    pass_on(0, 1)
    pass_on(0, 3)
    split(8, 12)
    piece_from(2)
    piece_from(6)
    pass_on(0, 2)
    split(12, 16)
    piece_from(3)
    piece_from(5)
    piece_from(4)
    split(16, 20)
    pass_on(1, 1)
    pass_on(1, 3)
    split(20, 26)
    pass_on(1, 2)
    split(26, 32)

    def panel_half(h):
        arrived(half(h, twin), S_A1 + 4 * h)
        for d in range(1, 4):
            origin = x_at(4 - d) * 2 + (1 - core)
            arrived(half(h, origin), S_A2 + 4 * h + d)

    def panel_rows(k0, k1):
        return jnp.concatenate([pt[k].reshape(256, 256) for k in range(k0, k1)], axis=1)

    panel_half(0)
    q_sum[...] = nn(panel_rows(0, 4), gs[0:1024, :])
    panel_half(1)

    def column_tile(j):
        columns = pl.ds(pl.multiple_of(j * 256, 256), 256)
        total = (q_sum[:, columns] + nn(panel_rows(4, 8), gs[1024:2048, columns])).astype(BF)
        q_bf[j] = total
        return nn(k_hi[...], total) + nn(k_lo[...], total)

    def column_half(d, h):
        rows = pl.ds(128 * h, 128)
        send(n_send.at[d, rows], e1.at[d, rows], S_E1 + 4 * h + d, row_y(d), col)

    for d in (2, 1, 3):
        n_send[d] = column_tile((y + d) % 4).astype(BF)
        column_half(d, 0)
    for d in (2, 1, 3):
        column_half(d, 1)
    n_own[...] = column_tile(y)

    for d in range(1, 4):
        arrived(tp.at[(y + 4 - d) % 4], S_B3 + d)

    def top_columns():
        return jnp.concatenate([tp[j].reshape(256, 256) for j in range(4)], axis=1)

    def column_sum(t, carry):
        rows = pl.ds(pl.multiple_of(t * 512, 512), 512)
        r_bf[rows, :] = nt(gs[rows, :], top_columns()).astype(BF)
        return carry

    q_all = jnp.concatenate([q_bf[j] for j in range(4)], axis=1)
    w[...] = (nt(q_all, top_columns()) + nt(top_columns(), q_all)).reshape(4, 2, 32, 256)
    send(w.at[:, 1 - core], wd, S_WC, row, twin)
    lax.fori_loop(0, 4, column_sum, 0)

    def k_tile(k, carry):
        rows = pl.ds(pl.multiple_of(k * 256, 256), 256)
        value = nt(k_hi[...], r_bf[rows, :]) + nt(k_lo[...], r_bf[rows, :])
        mst[k] = value.reshape(4, 2, 32, 256).astype(BF)
        return carry

    def core_half(h):
        send(mst.at[pl.ds(4 * h, 4), :, 1 - core], d1.at[pl.ds(4 * h, 4)], S_D1 + h, row, twin)

    def join(h):
        arrived(d1.at[pl.ds(4 * h, 4)], S_D1 + h)
        for other in range(4):
            for k in range(4 * h, 4 * h + 4):
                cmb[other, k] = (mst[k, other, core].astype(F32) + d1[k, other].astype(F32)).astype(BF)
        for d in (1, 3, 2):
            part = pl.ds(4 * h, 4)
            send(cmb.at[x_at(d), part], d2.at[d, part], S_D2 + 4 * h + d, row, col_at(d))

    def strips_out(h):
        rows = pl.ds(128 * h, 128)
        total = n_own[rows, :]
        for d in range(1, 4):
            arrived(e1.at[d, rows], S_E1 + 4 * h + d)
            total += e1[d, rows, :].astype(F32)
        n_own[rows, :] = total
        e2s[pl.ds(4 * h, 4)] = total.reshape(4, 32, 256).astype(BF)
        for other in range(4 * h, 4 * h + 4):

            @pl.when(z != other)
            def _():
                remote(e2s.at[other], e2r.at[z], S_E2 + other, S_E2 + z, y * 8 + other, col).start()

    arrived(wd, S_WC)
    wc[...] = w[:, core] + wd[...]
    for d in (2, 1, 3):
        send(wc.at[x_at(d)], wx.at[d], S_WX + d, row, col_at(d))

    lax.fori_loop(0, 4, k_tile, 0)
    core_half(0)
    lax.fori_loop(4, 8, k_tile, 0)
    core_half(1)
    join(0)
    strips_out(0)
    for d in range(1, 4):
        arrived(wx.at[d], S_WX + d)
    total = (wc[x] + wx[1] + wx[2] + wx[3]).astype(BF)
    wy[y] = total
    for d in (2, 1, 3):
        send(wy.at[y], wy.at[y], S_WY + d, row_y(d), col)
    strips_out(1)
    join(1)

    def top_tile(j, carry):
        tile = tp[j].reshape(256, 256)
        topt[j] = (nn(inv_hi[...], tile) + nn(inv_lo[...], tile)).astype(BF)
        return carry

    def factor_tile(k, carry):
        tile = pt[k].reshape(256, 256)
        fn[k] = (nn(inv_hi[...], tile) + nn(inv_lo[...], tile)).T.astype(BF)
        return carry

    lax.fori_loop(0, 4, top_tile, 0)
    lax.fori_loop(0, 8, factor_tile, 0)

    for d in range(1, 4):
        arrived(wy.at[(y + 4 - d) % 4], S_WY + d)
    total = wy[0].astype(F32)
    for k in range(1, 4):
        total += wy[k].astype(F32)
    wz[z] = total.astype(BF)
    for d in (4, 3, 5, 2, 6, 1, 7):
        send(wz.at[z], wz.at[z], S_WZ + d, row_z(d), col)

    for d in range(1, 8):
        origin = (z + 8 - d) % 8
        arrived(e2r.at[origin], S_E2 + origin)
    e2r[z] = jnp.zeros((32, 256), BF)
    total = n_own[pl.ds(pl.multiple_of(z * 32, 32), 32), :]
    for k in range(8):
        total += e2r[k].astype(F32)
    e3s[...] = total.astype(BF)
    e3_out = remote(e3s, e3, S_E3, S_E3, mirror, z)

    @pl.when(jnp.logical_not(is_root))
    def _():
        e3_out.start()

    in_slab.wait()

    def out_rows(k):
        rows = pl.ds(pl.multiple_of(k * 256, 256), 256)
        return pltpu.make_async_copy(sraw.at[rows], upd_ref.at[rows], lsem.at[4 + k])

    def update_tile(k, carry):
        start = pl.multiple_of(k * 256, 256)
        products = [nn(fn[k], topt[j]).astype(BF) for j in range(4)]
        for t in range(4):
            rows = pl.ds(pl.multiple_of(start + t * 64, 64), 64)
            product = jnp.concatenate([products[j][t * 64 : (t + 1) * 64] for j in range(4)], axis=0)
            old = sraw[rows].reshape(256, 256).astype(F32)
            sraw[rows] = (old - nn(permt[...], product)).astype(BF).reshape(64, 4, 256)
        out_rows(k).start()
        return carry

    lax.fori_loop(0, 8, update_tile, 0)

    for h in range(2):
        for d in range(1, 4):
            arrived(d2.at[d, pl.ds(4 * h, 4)], S_D2 + 4 * h + d)
    for k in range(1, 8):
        value = mst[k, x, core].astype(F32) + d1[k, x].astype(F32)
        for d in range(1, 4):
            value += d2[d, k].astype(F32)
        gpo[k] = -value

    @pl.when(is_root)
    def _():
        e3[...] = e3s[...]

    @pl.when(jnp.logical_not(is_root))
    def _():
        arrived(e3, S_E3)

    value = mst[0, x, core].astype(F32) + d1[0, x].astype(F32) + e3[...].astype(F32)
    for d in range(1, 4):
        value += d2[d, 0].astype(F32)
    gpo[0] = -value
    out_gp = pltpu.make_async_copy(gpo, gp_ref, lsem.at[12])
    out_gp.start()

    for d in range(1, 8):
        arrived(wz.at[(z + 8 - d) % 8], S_WZ + d)
    total = wz[0].astype(F32)
    for k in range(1, 8):
        total += wz[k].astype(F32)
    high, low = halves(total)
    gio[...] = -three(high, low, inv_hi[...], inv_lo[...], nt)
    out_gi = pltpu.make_async_copy(gio, gi_ref, lsem.at[13])
    out_gi.start()

    @pl.when(jnp.logical_not(is_root))
    def _():
        strip_to(0).wait_send()
        e3_out.wait_send()

    for d in range(1, 8):
        strip_to(d).wait_send()

    for d in range(1, 4):
        remote(tp.at[y], tp.at[y], S_B3 + d, S_B3 + d, row_y(d), col).wait_send()
    for other in range(8):

        @pl.when(z != other)
        def _():
            remote(e2s.at[other], e2r.at[z], S_E2 + other, S_E2 + z, y * 8 + other, col).wait_send()

    for copy in sent:
        copy.wait_send()
    for k in range(8):
        out_rows(k).wait()
    out_gp.wait()
    out_gi.wait()


def per_device(panel, slab, cotangent, inverse):
    strips = jnp.transpose(panel.reshape(8, 256, 32), (0, 2, 1))
    vmem = pltpu.VMEM
    updated, grad_panel, grad_inverse = pl.pallas_call(
        kernel,
        out_shape=(
            jax.ShapeDtypeStruct((2048, 4, 256), BF),
            jax.ShapeDtypeStruct((8, 32, 256), F32),
            jax.ShapeDtypeStruct((32, 256), F32),
        ),
        in_specs=[pl.BlockSpec(memory_space=pltpu.HBM)] * 4,
        out_specs=[pl.BlockSpec(memory_space=pl.ANY)] * 3,
        scratch_shapes=[
            vmem((8, 32, 256), F32), vmem((256, 256), F32),
            vmem((256, 256), BF), vmem((256, 256), BF), vmem((256, 256), BF), vmem((256, 256), BF),
            vmem((256, 256), BF), vmem((256, 256), BF),
            vmem((2048, 4, 256), BF), vmem((2048, 1024), BF), vmem((2048, 4, 256), BF),
            vmem((8, 8, 32, 256), BF), vmem((8, 256, 256), BF),
            vmem((4, 8, 32, 256), BF), vmem((4, 256, 256), BF),
            vmem((256, 1024), F32), vmem((4, 256, 256), BF), vmem((256, 256), F32),
            vmem((4, 256, 256), BF), vmem((4, 256, 256), BF),
            vmem((8, 32, 256), BF), vmem((8, 32, 256), BF),
            vmem((32, 256), BF), vmem((32, 256), BF),
            vmem((2048, 256), BF), vmem((4, 2, 32, 256), F32),
            vmem((8, 4, 2, 32, 256), BF), vmem((8, 4, 32, 256), BF),
            vmem((4, 8, 32, 256), BF), vmem((4, 8, 32, 256), BF),
            vmem((4, 32, 256), F32), vmem((4, 32, 256), F32), vmem((4, 32, 256), F32),
            vmem((4, 32, 256), BF), vmem((8, 32, 256), BF),
            vmem((8, 32, 256), F32), vmem((32, 256), F32),
            pltpu.SemaphoreType.DMA((N_SEM,)), pltpu.SemaphoreType.DMA((N_SEM,)), pltpu.SemaphoreType.DMA((14,)),
        ],
        compiler_params=pltpu.CompilerParams(
            collective_id=0, has_side_effects=True, vmem_limit_bytes=48 << 20
        ),
    )(pltpu.with_memory_space_constraint(strips, pltpu.HBM), slab.reshape(2048, 4, 256), cotangent.reshape(2048, 4, 256), pltpu.with_memory_space_constraint(inverse, pltpu.HBM))
    return (
        updated.reshape(slab.shape),
        jnp.transpose(grad_panel, (0, 2, 1)).reshape(panel.shape),
        jnp.transpose(grad_inverse),
    )


def solution(mesh):
    in_specs = (
        P(None, "row", None, "col"),
        P(None, "row", None, None, "col", None),
        P(None, "row", None, None, "col", None),
        P(),
    )
    out_specs = (
        P(None, "row", None, None, "col", None),
        P(None, "row", None, "col"),
        P(None, "col"),
    )
    return jax.shard_map(
        per_device, mesh=mesh, in_specs=in_specs, out_specs=out_specs, check_vma=False
    )
```
